32 devices in a mesh: rows: 2 (over core), waves: 16 (over z, y, x).
Axes of the slice: x: 2, y: 2, z: 4, core: 2. Of those that a mesh axis runs over, the one named last changes fastest.
Arguments:
- feats: float32 [8192, 256], P(('rows', 'waves')), may hold values from -6 to 6
- positions: float32 [3, 8192], P(None, ('rows', 'waves')), may hold values from 0 to 6
- cell_counts: int32 [64], P(('rows', 'waves')), may hold values from 1 to 128
- neighbours: int32 [64, 5], P(('rows', 'waves')), may hold values from 0 to 63, as said below
- nbr_count: int32 [64], P(('rows', 'waves')), may hold values from 3 to 5
- kvec: float32 [3, 3072], P(None, 'waves'), may hold values from -4 to 4
- filters: float32 [3072, 256], P('waves'), may hold values from -5 to 5
- w_msg: float32 [256, 256], replicated, may hold values from -0.375 to 0.375
- w_val: float32 [256, 256], replicated, may hold values from -0.375 to 0.375
- w_one: float32 [256, 256], replicated, may hold values from -0.375 to 0.375
- w_two: float32 [256, 256], replicated, may hold values from -0.375 to 0.375
Outputs:
- updated: float32 [8192, 256], P(('rows', 'waves'))
The draws below stay inside these ranges and needn't reach their ends.
Inputs may be any that keep to these rules, and one draw needn't show every extreme that they name: `neighbours`: column 0 of each cell's list is the cell itself, column 1 the cell (c - 2) mod 64, column 2 the cell (c + 2) mod 64; the 5 entries of a list are distinct cells, and every listed cell c' of cell c satisfies (c' - c) mod 64 <= 2 or (c - c') mod 64 <= 2; entries at or beyond nbr_count are in range and unused.
All inputs are finite; a program needn't handle non-finite values.
Results may differ from the reference program's by a relative error of at most 0.0003.
Values sent between devices are 32-bit elements; how exact they have to be, the bound alone decides.
A program may use at most 128 MiB of HBM per device.

```python
import jax
import jax.numpy as jnp
from jax import lax

F = 256
CELL = 128
NB = 5
KWAVES = 3072
CELLS_DEV = 2
CELLS = 64
SLOTS = 8192
DEVICES = 32


def draw_neighbours(key, part):
    span = 2 * CELLS_DEV + 1
    offs = jnp.arange(span, dtype=jnp.int32) - CELLS_DEV
    scores = jax.random.randint(jax.random.fold_in(key, 17), (CELLS, span), 0, 1 << 20)
    scores = scores * span + jnp.arange(span, dtype=jnp.int32)[None, :]
    scores = jnp.where(offs[None, :] == 0, jnp.int32(3 << 28), scores)
    scores = jnp.where(offs[None, :] == -CELLS_DEV, jnp.int32(2 << 28), scores)
    scores = jnp.where(offs[None, :] == CELLS_DEV, jnp.int32(1 << 28), scores)
    order = jnp.argsort(-scores, axis=1, stable=True)[:, :NB]
    chosen = offs[order]
    own = jnp.arange(CELLS, dtype=jnp.int32)[:, None]
    return ((own + chosen) % CELLS).astype(jnp.int32)


def set_ends(entries, rng, low, high):
    longest = entries.shape.index(max(entries.shape))
    spots = []
    for shift in (0, 1):
        where = [jax.random.randint(jax.random.fold_in(rng, axis), (), 0, length) for axis, length in enumerate(entries.shape)]
        where[longest] = (where[longest] + shift) % entries.shape[longest]
        spots.append(tuple(where))
    return entries.at[spots[0]].set(low).at[spots[1]].set(high)


def shard_levels(key, shape, pieces, low, top_value):
    loudness, own = 1.0, jax.random.fold_in(key, 6)
    for dim, blocks in pieces:
        steps = jnp.exp(jax.random.uniform(jax.random.fold_in(own, dim), (blocks,), jnp.float32, low / len(pieces), top_value / len(pieces)))
        loudness = loudness * jnp.repeat(steps, shape[dim] // blocks).reshape([-1 if axis == dim else 1 for axis in range(len(shape))])
    return loudness


def scatter_about(stream_key, shape, deviation, most, split=(), held_as=jnp.bfloat16):
    result = deviation * jax.random.normal(stream_key, shape, jnp.float32)
    if split:
        result = result * shard_levels(stream_key, shape, split, -0.22, 0.18)
    return jnp.clip(result, -most, most).astype(held_as)


def setup_inputs(seed: int = 0) -> dict:
    seeds = jax.random.split(jax.random.key(seed), 12)
    feats = scatter_about(seeds[0], (SLOTS, F), 1.0, 6.0, ((0, 32),), jnp.float32)
    positions = jnp.clip(6.0 * jax.random.uniform(seeds[1], (3, SLOTS), jnp.float32) ** shard_levels(seeds[1], (3, SLOTS), ((1, 32),), -0.2, 0.2), 0.0, 6.0)
    cell_counts = set_ends(jax.random.randint(seeds[2], (CELLS,), 1, CELL + 1), jax.random.fold_in(seeds[2], 1), 1, CELL).astype(jnp.int32)
    neighbours = draw_neighbours(jax.random.fold_in(seeds[11], 71), 0)
    nbr_count = set_ends(jax.random.randint(seeds[4], (CELLS,), 3, NB + 1), jax.random.fold_in(seeds[4], 1), 3, NB).astype(jnp.int32)
    kvec = scatter_about(seeds[5], (3, KWAVES), 1.0, 4.0, ((1, 16),), jnp.float32)
    filters = scatter_about(seeds[6], (KWAVES, F), 1.0, 5.0, ((0, 16),), jnp.float32)
    w_msg = scatter_about(seeds[7], (F, F), F ** -0.5, 0.375, (), jnp.float32)
    w_val = scatter_about(seeds[8], (F, F), F ** -0.5, 0.375, (), jnp.float32)
    w_one = scatter_about(seeds[9], (F, F), F ** -0.5, 0.375, (), jnp.float32)
    w_two = scatter_about(seeds[10], (F, F), F ** -0.5, 0.375, (), jnp.float32)
    return {"feats": feats, "positions": positions, "cell_counts": cell_counts, "neighbours": neighbours, "nbr_count": nbr_count, "kvec": kvec, "filters": filters, "w_msg": w_msg, "w_val": w_val, "w_one": w_one, "w_two": w_two}


HIGH = lax.Precision.HIGHEST

def reference(feats, positions, cell_counts, neighbours, nbr_count, kvec, filters, w_msg, w_val, w_one, w_two):
    slot_ids = jnp.arange(CELL, dtype=jnp.int32)
    valid2 = (slot_ids[None, :] < cell_counts[:, None]).astype(jnp.float32)
    valid = valid2.reshape(-1)
    hw = jnp.dot(feats, w_msg, precision=HIGH)
    vals = jnp.dot(feats, w_val, precision=HIGH) * valid[:, None]
    pos3 = positions.reshape(3, CELLS, CELL)
    hw3 = hw.reshape(CELLS, CELL, F)
    same_slot = jnp.eye(CELL, dtype=jnp.bool_)

    def one_cell(c):
        own = pos3[:, c]
        acc = jnp.zeros((CELL, F), jnp.float32)
        for b in range(NB):
            other = neighbours[c, b]
            near = pos3[:, other]
            dist = lax.optimization_barrier(jnp.sum((own[:, :, None] - near[:, None, :]) ** 2, axis=0))
            live = (b < nbr_count[c]).astype(jnp.float32)
            keep = valid2[c][:, None] * valid2[other][None, :] * live
            weight = jnp.where(same_slot & (other == c), 0.0, jnp.exp(-0.125 * dist) * keep)
            acc = acc + jnp.dot(weight, hw3[other], precision=HIGH)
        return acc
    msg = 0.125 * lax.map(one_cell, jnp.arange(CELLS, dtype=jnp.int32)).reshape(SLOTS, F)
    block = SLOTS // DEVICES
    pos_blocks = positions.reshape(3, DEVICES, block).transpose(1, 0, 2)
    val_blocks = vals.reshape(DEVICES, block, F)

    def forward(carry, item):
        pos_b, val_b = item
        phase = jnp.dot(kvec.T, pos_b, precision=HIGH)
        return ((carry[0] + jnp.dot(jnp.cos(phase), val_b, precision=HIGH), carry[1] + jnp.dot(jnp.sin(phase), val_b, precision=HIGH)), None)
    zero = jnp.zeros((KWAVES, F), jnp.float32)
    (sum_cos, sum_sin), _ = lax.scan(forward, (zero, zero), (pos_blocks, val_blocks))
    filt_cos = filters * sum_cos
    filt_sin = filters * sum_sin

    def backward(pos_b):
        phase = jnp.dot(pos_b.T, kvec, precision=HIGH)
        return jnp.dot(jnp.cos(phase), filt_cos, precision=HIGH) + jnp.dot(jnp.sin(phase), filt_sin, precision=HIGH)
    ewald = lax.map(backward, pos_blocks).reshape(SLOTS, F) / jnp.sqrt(jnp.float32(SLOTS) * jnp.float32(KWAVES))
    total = feats + msg + ewald
    normed = total / jnp.sqrt(lax.optimization_barrier(jnp.mean(total * total, axis=1, keepdims=True)) + 1e-06)
    hidden = jax.nn.silu(jnp.dot(normed, w_one, precision=HIGH))
    return (total + jnp.dot(hidden, w_two, precision=HIGH)) * valid[:, None]
```

```python
import functools
import math

import jax
import jax.numpy as jnp
from jax import lax
from jax.experimental import pallas as pl
from jax.experimental.pallas import tpu as pltpu
from jax.sharding import PartitionSpec as P

MESH = pl.DeviceIdType.MESH
F32 = jnp.float32
BF16 = jnp.bfloat16

SIN = (4.44286798, -7.30744541, 3.5948021, -0.78440363)
COS = (1.4142135, -6.97885099, 5.73946117, -1.88356299, 0.31069819)


def split(x):
    high = x.astype(BF16)
    return high, (x - high.astype(F32)).astype(BF16)


def split3(x):
    a = x.astype(BF16).astype(F32)
    rest = x - a
    b = rest.astype(BF16).astype(F32)
    return a, b, rest - b


def mm(a, b):
    return jnp.dot(a, b, preferred_element_type=F32)


def dot3(a, b):
    return mm(a[0], b[0]) + mm(a[0], b[1]) + mm(a[1], b[0])


def horner(y, coefficients):
    total = y * coefficients[-1] + coefficients[-2]
    for coefficient in coefficients[-3::-1]:
        total = total * y + coefficient
    return total


def sincos(turns):
    x = turns - jnp.round(turns)
    y = x * x
    s = x * horner(y, SIN)
    c = horner(y, COS)
    return s * c, 1.0 - s * s


def columns(rows):
    height, width = rows.shape
    return jnp.concatenate([rows, jnp.zeros((128 - height, width), F32)], axis=0).T


def body(
    nz, plane, scale,
    counts, neigh, ncount, feats_in, pos_in, kv_in, filt_in, w_msg_in, w_val_in, w_one_in, w_two_in,
    out,
    feats, pos3, kv3, filt, w_msg, w_val, w_one, w_two,
    fm, pos, kv, vals, vals_all, pos_all, kv_all, near_feat, near_pos, km, ch, cl, sh, sl, fcat,
    s_acc, xbuf, zs, zr, f_all, fth, ftl, es, er, msg,
    s_in, s_pos, r_pos, s_val, r_val, s_near, r_near, s_kv, r_kv, s_x, r_x, s_z, r_z, s_f, r_f, s_g, s_e, r_e,
):
    slots, width = feats.shape
    kb = filt.shape[0]
    half = kb // 2
    hw = width // 2
    kall = nz * kb
    kpad = km.shape[0]
    cells = counts.shape[0]
    cell = slots // cells
    waves = nz * plane
    r = lax.axis_index("rows")
    w = lax.axis_index("waves")
    z = w // plane
    p = w % plane
    other = (1 - r, w)
    place = r * waves + w
    devices = 2 * waves
    scope = jax.named_scope

    def place_dev(q):
        return (q // waves, q % waves)

    prev_dev = place_dev((place + devices - 1) % devices)
    next_dev = place_dev((place + 1) % devices)

    def plane_dev(j):
        return (r, z * plane + (p + j) % plane)

    def z_dev(j):
        return (r, ((z + j) % nz) * plane + p)

    def rcopy(src, dst, ssem, rsem, dev):
        return pltpu.make_async_remote_copy(
            src_ref=src, dst_ref=dst, send_sem=ssem, recv_sem=rsem, device_id=dev, device_id_type=MESH
        )

    def rows_of(block):
        return pl.ds(pl.multiple_of(block * slots, slots), slots)

    loads = [
        pltpu.make_async_copy(src, dst, s_in.at[i])
        for i, (src, dst) in enumerate(
            (
                (pos_in, pos3),
                (kv_in, kv3),
                (feats_in, feats),
                (w_val_in, w_val),
                (filt_in, filt),
                (w_msg_in, w_msg),
                (w_one_in, w_one),
                (w_two_in, w_two),
            )
        )
    ]
    for load in loads:
        load.start()

    barrier = pltpu.get_barrier_semaphore()
    for dev in (other, prev_dev, next_dev):
        pl.semaphore_signal(barrier, inc=1, device_id=dev, device_id_type=MESH)
    for j in range(1, nz):
        pl.semaphore_signal(barrier, inc=1, device_id=z_dev(j), device_id_type=MESH)

    @pl.loop(1, plane)
    def _(j):
        pl.semaphore_signal(barrier, inc=1, device_id=plane_dev(j), device_id_type=MESH)

    with scope("A_load"):
        loads[0].wait()
        loads[1].wait()
        pos[...] = jnp.zeros_like(pos)
        pos[0:3, :] = pos3[...]
        kv[...] = jnp.zeros_like(kv)
        kv[0:3, 0:kb] = kv3[...] * (0.5 / math.pi)
        loads[2].wait()
        slot_ids = lax.broadcasted_iota(jnp.int32, (cell, width), 0)
        for c in range(cells):
            part = slice(c * cell, (c + 1) * cell)
            fm[part, :] = jnp.where(slot_ids < counts[c], feats[part, :], 0.0)
        loads[3].wait()
        projected = dot3(split(fm[...]), split(w_val[...]))
        for h in range(2):
            vals[h] = projected[:, h * hw : (h + 1) * hw]

    with scope("A_barrier"):
        pl.semaphore_wait(barrier, nz + plane + 1)

    def kv_copy(j):
        return rcopy(kv, kv_all.at[z], s_kv.at[j], r_kv.at[z], z_dev(j))

    def kv_arrival(j):
        q = (z + j) % nz
        return rcopy(kv, kv_all.at[q], s_kv.at[j], r_kv.at[q], z_dev(j))

    def pos_copy(j):
        return rcopy(pos, pos_all.at[p], s_pos.at[j], r_pos.at[p], plane_dev(j))

    def pos_arrival(q):
        return rcopy(pos, pos_all.at[q], s_pos.at[0], r_pos.at[q], other)

    def val_copy(h, j):
        return rcopy(vals.at[h], vals_all.at[h, p], s_val.at[h, j], r_val.at[h, p], plane_dev(j))

    def val_arrival(h, q):
        return rcopy(vals.at[h], vals_all.at[h, q], s_val.at[h, 0], r_val.at[h, q], other)

    def near_copies(side):
        dev = next_dev if side == 0 else prev_dev
        return (
            rcopy(pos, near_pos.at[side], s_near.at[side, 0], r_near.at[side, 0], dev),
            rcopy(fm, near_feat.at[side], s_near.at[side, 1], r_near.at[side, 1], dev),
        )

    for j in range(1, nz):
        kv_copy(j).start()

    @pl.loop(1, plane)
    def _(j):
        pos_copy(j).start()

    for h in range(2):

        @pl.loop(1, plane)
        def _(j):
            val_copy(h, j).start()

    for side in range(2):
        for copy in near_copies(side):
            copy.start()

    def place_k(block, rows):
        a, b, c = split3(rows)
        stack = [a, a, a, b, b, b, c, c, c]
        stack.append(jnp.zeros((128 - 8 * len(stack), rows.shape[1]), F32))
        km[pl.ds(pl.multiple_of(block * kb, 16), kb), :] = jnp.concatenate(stack, axis=0).T[:kb].astype(BF16)

    def place_v(h, q, block):
        a, b = split(block)
        fcat[h, rows_of(q), 0:hw] = a
        fcat[h, rows_of(q), hw:width] = b

    if kpad > kall:
        f_all[:, :, kall:, :] = jnp.zeros((2, 2, kpad - kall, hw), F32)
    for h in range(2):
        place_v(h, p, vals[h])
    with scope("B_kv"):
        place_k(z, kv[...])
        if kpad > kall:
            km[kall:, :] = jnp.zeros((kpad - kall, 128), BF16)
        for j in range(1, nz):
            kv_arrival(j).wait_recv()
            q = (z + j) % nz
            place_k(q, kv_all[q])

    def phases(q, rows3):
        stack = list(split3(rows3)) * 3
        stack.append(jnp.zeros((128 - 8 * len(stack), slots), F32))
        s, c = sincos(mm(km[...], jnp.concatenate(stack, axis=0).astype(BF16)))
        lanes = rows_of(q)
        a, b = split(c)
        ch[:, lanes] = a
        cl[:, lanes] = b
        a, b = split(s)
        sh[:, lanes] = a
        sl[:, lanes] = b

    pos_all[p] = pos[...]

    with scope("C_phases"):

        @pl.loop(0, plane)
        def _(j):
            q = (p + j) % plane

            @pl.when(j > 0)
            def _():
                pos_arrival(q).wait_recv()

            phases(q, pos_all[q])

    natoms = plane * slots
    lower = z < nz // 2
    rank = jnp.where(lower, z, nz - 1 - z)
    ahead = jnp.where(lower, 0, 1)
    inner = rank > 0

    def block_at(j):
        far = nz - 1 - rank
        block = jnp.where(j < far, nz - 1 - j, j - far)
        return jnp.where(lower, block, nz - 1 - block)

    def partial_sums(h, j):
        zb = block_at(j)
        ks = pl.ds(pl.multiple_of(zb * kb, 16), kb)
        for part, (hi, lo) in enumerate(((ch, cl), (sh, sl))):
            wide = mm(hi[ks, :], fcat[h])
            total = wide[:, :hw] + wide[:, hw:] + mm(lo[ks, :], fcat[h, :, 0:hw])
            for c in range(2):
                s_acc[h, zb, c, part] = total[c * half : (c + 1) * half]

    def x_copy(h, j):
        zb = block_at(j)
        return rcopy(s_acc.at[h, zb, 1 - r], xbuf.at[h, zb], s_x.at[h, zb], r_x.at[h, zb], other)

    def step(way):
        return (r, (z + 1 - 2 * way) * plane + p)

    def s_hop(h, zb, part, way):
        return rcopy(
            zs.at[h, zb, part], zr.at[way, h, zb, part], s_z.at[h, zb, part], r_z.at[way, h, zb, part], step(way)
        )

    def add_arrival(h, zb, part, way):
        s_hop(h, zb, part, way).wait_recv()
        zs[h, zb, part] = zs[h, zb, part] + zr[way, h, zb, part]

    def pass_on(h, j):
        zb = block_at(j)
        x_copy(h, j).wait_recv()
        forward = j < nz - 1 - rank
        for part in range(2):
            zs[h, zb, part] = s_acc[h, zb, r, part] + xbuf[h, zb, part]
        for part in range(2):

            @pl.when(inner & (forward | (j == nz - 1)))
            def _():
                add_arrival(h, zb, part, ahead)

            @pl.when(jnp.logical_not(forward))
            def _():
                add_arrival(h, zb, part, 1 - ahead)

            if j < nz - 1:
                s_hop(h, zb, part, jnp.where(forward, ahead, 1 - ahead)).start()

    def share(h, part, zb, c):
        return f_all.at[h, part, pl.ds(pl.multiple_of((zb * 2 + c) * half, 8), half), :]

    def f_hop(h, part, zb, way, d):
        here = share(h, part, zb, r)
        return rcopy(here, here, s_f.at[h, part, way, d], r_f.at[h, part, zb, r], step(way))

    def f_relay(h, part, zb):
        here = share(h, part, zb, r)
        return rcopy(here, here, s_g.at[h, part, zb], r_f.at[h, part, zb, r], other)

    def f_arrival(h, part, zb, c):
        here = share(h, part, zb, c)
        return rcopy(here, here, s_g.at[h, part, zb], r_f.at[h, part, zb, c], other)

    mine = pl.multiple_of(r * half, 8)

    def f_own(h):
        own_filter = filt[pl.ds(mine, half), h * hw : (h + 1) * hw] * scale
        for part in range(2):
            f_all[h, part, pl.ds(pl.multiple_of((z * 2 + r) * half, 8), half), :] = own_filter * zs[h, z, part]
            for way, more in ((0, z < nz - 1), (1, z > 0)):

                @pl.when(more)
                def _():
                    f_hop(h, part, z, way, 0).start()

            f_relay(h, part, z).start()

    def f_pass(h, d):
        for part in range(2):
            for way, there, more in ((0, z >= d, z < nz - 1), (1, z + d < nz, z > 0)):
                zb = z - d if way == 0 else z + d

                @pl.when(there)
                def _():
                    f_arrival(h, part, zb, r).wait_recv()

                @pl.when(there & more)
                def _():
                    f_hop(h, part, zb, way, d).start()

                @pl.when(there)
                def _():
                    f_relay(h, part, zb).start()

    def back(h, q):
        lanes = rows_of(q)
        return dot3((fth[h, 0], ftl[h, 0]), (ch[:, lanes], cl[:, lanes])) + dot3(
            (fth[h, 1], ftl[h, 1]), (sh[:, lanes], sl[:, lanes])
        )

    def e_copy(h, j):
        return rcopy(es.at[h, j], er.at[h, j], s_e.at[h, j], r_e.at[h, j], plane_dev(j))

    def gather_half(h):
        for part in range(2):
            for zb in range(nz):
                f_arrival(h, part, zb, 1 - r).wait_recv()
            a, b = split(f_all[h, part].T)
            fth[h, part] = a
            ftl[h, part] = b

    def back_range(h, start, stop):
        @pl.loop(start, stop)
        def _(j):
            es[h, j] = back(h, (p + j) % plane)
            e_copy(h, j).start()

    def take_vals(h):
        @pl.loop(1, plane)
        def _(j):
            q = (p + j) % plane
            val_arrival(h, q).wait_recv()
            place_v(h, q, vals_all[h, q])

    def own_message():
        first = place * cells
        total_cells = cells * devices
        own_cols = columns(pos[...])
        same = lax.broadcasted_iota(jnp.int32, (slots, slots), 0) == lax.broadcasted_iota(
            jnp.int32, (slots, slots), 1
        )
        row_cell = lax.broadcasted_iota(jnp.int32, (slots, slots), 0) // cell
        col_cell = lax.broadcasted_iota(jnp.int32, (slots, slots), 1) // cell

        def listed(c, target):
            found = jnp.float32(0.0)
            for b in range(neigh.shape[1]):
                hit = (neigh[c, b] == target) & (b < ncount[c])
                found = found + jnp.where(hit, 1.0, 0.0)
            return found

        gathered = jnp.zeros((slots, width), F32)
        for shift in (-1, 0, 1):
            if shift:
                for copy in near_copies(0 if shift < 0 else 1):
                    copy.wait_recv()
            near = pos[...] if shift == 0 else near_pos[0 if shift < 0 else 1]
            atoms = fm[...] if shift == 0 else near_feat[0 if shift < 0 else 1]
            dist = jnp.zeros((slots, slots), F32)
            for axis in range(3):
                diff = own_cols[:, axis : axis + 1] - near[axis : axis + 1]
                dist = dist + diff * diff
            live = jnp.zeros((slots, slots), F32)
            for c in range(cells):
                for t in range(cells):
                    target = (first + shift * cells + t + total_cells) % total_cells
                    live = jnp.where((row_cell == c) & (col_cell == t), listed(c, target), live)
            weight = jnp.exp(-0.125 * dist) * live
            if shift == 0:
                weight = jnp.where(same, 0.0, weight)
            gathered = gathered + dot3(split(weight), split(atoms))
        msg[...] = feats[...] + 0.125 * dot3(split(gathered), split(w_msg[...]))

    with scope("D_takeA"):
        take_vals(0)
    with scope("D_psumA"):
        for j in range(nz):
            partial_sums(0, j)
            x_copy(0, j).start()
            if j:

                @pl.when(jnp.logical_not(inner))
                def _():
                    pass_on(0, j - 1)

    with scope("D_passA01"):

        @pl.when(inner)
        def _():
            for j in range(nz // 2):
                pass_on(0, j)

    with scope("E_takeB"):
        take_vals(1)
    with scope("E_psumB"):
        for j in range(nz):
            partial_sums(1, j)
            x_copy(1, j).start()
            if j:

                @pl.when(jnp.logical_not(inner))
                def _():
                    pass_on(1, j - 1)

    with scope("E_passA2"):

        @pl.when(inner)
        def _():
            for j in range(nz // 2, nz - 1):
                pass_on(0, j)

    for load in loads[4:]:
        load.wait()
    with scope("F_passA3"):
        pass_on(0, nz - 1)
    with scope("F_ownA"):
        f_own(0)
    with scope("F_msg"):
        own_message()
    with scope("G_passB01"):

        @pl.when(inner)
        def _():
            for j in range(nz // 2):
                pass_on(1, j)

    with scope("G_fpassA1"):
        f_pass(0, 1)
    with scope("G_passB2"):

        @pl.when(inner)
        def _():
            for j in range(nz // 2, nz - 1):
                pass_on(1, j)

    with scope("G_fpassA2e"):

        @pl.when(jnp.logical_not(inner))
        def _():
            for d in range(2, nz - 1):
                f_pass(0, d)

    with scope("H_passB3"):
        pass_on(1, nz - 1)
    with scope("H_ownB"):
        f_own(1)
    with scope("H_fpassA2i"):

        @pl.when(inner)
        def _():
            for d in range(2, nz - 1):
                f_pass(0, d)

        if nz > 2:
            f_pass(0, nz - 1)
    with scope("I_gatherA"):
        gather_half(0)
    with scope("I_backA"):
        back_range(0, 1, plane)
    with scope("J_fpassB"):
        for d in range(1, nz):
            f_pass(1, d)
    with scope("K_gatherB"):
        gather_half(1)
    with scope("K_backB"):
        back_range(1, 1, plane)
    with scope("L_own"):
        for h in range(2):
            es[h, 0] = back(h, p)

    with scope("M_ewait"):
        for h in range(2):

            @pl.loop(1, plane)
            def _(j):
                e_copy(h, j).wait_recv()
                es[h, 0] = es[h, 0] + er[h, j]

    with scope("N_mlp"):
        summed = msg[...] + jnp.concatenate([es[0, 0].T, es[1, 0].T], axis=1)
        normed = summed / jnp.sqrt(jnp.mean(summed * summed, axis=1, keepdims=True) + 1e-06)
        v = dot3(split(normed), split(w_one[...]))
        hidden = v / (1.0 + jnp.exp(-v))
        result = summed + dot3(split(hidden), split(w_two[...]))
        for c in range(cells):
            part = slice(c * cell, (c + 1) * cell)
            out[part, :] = jnp.where(slot_ids < counts[c], result[part], 0.0)

    for j in range(1, nz):
        kv_copy(j).wait_send()
    for h in range(2):
        for j in range(nz):
            x_copy(h, j).wait_send()
            if j < nz - 1:
                for part in range(2):
                    s_hop(h, block_at(j), part, 0).wait_send()
        for part in range(2):
            for zb in range(nz):
                f_relay(h, part, zb).wait_send()
            for d in range(nz):
                for way, there, more in ((0, z >= d, z < nz - 1), (1, z + d < nz, z > 0)):

                    @pl.when(there & more)
                    def _():
                        f_hop(h, part, z - d if way == 0 else z + d, way, d).wait_send()

    @pl.loop(1, plane)
    def _(j):
        pos_copy(j).wait_send()
        for h in range(2):
            val_copy(h, j).wait_send()
            e_copy(h, j).wait_send()

    for side in range(2):
        for copy in near_copies(side):
            copy.wait_send()


def shards(
    nz, feats, positions, cell_counts, neighbours, nbr_count, kvec, filters, w_msg, w_val, w_one, w_two
):
    slots, width = feats.shape
    kb = kvec.shape[1]
    waves = lax.axis_size("waves")
    plane = waves // nz
    devices = lax.axis_size("rows") * waves
    kpad = -(-nz * kb // 128) * 128
    kbpad = -(-kb // 128) * 128
    half = kb // 2
    hw = width // 2
    scale = 1.0 / math.sqrt(float(slots * devices) * float(kb * waves))
    natoms = plane * slots
    vm = pltpu.VMEM
    dma = pltpu.SemaphoreType.DMA
    smem_spec = pl.BlockSpec(memory_space=pltpu.SMEM)
    any_spec = pl.BlockSpec(memory_space=pl.ANY)
    vmem_spec = pl.BlockSpec(memory_space=pltpu.VMEM)
    return pl.pallas_call(
        functools.partial(body, nz, plane, scale),
        out_shape=jax.ShapeDtypeStruct((slots, width), F32),
        in_specs=[smem_spec] * 3 + [any_spec] * 8,
        out_specs=vmem_spec,
        scratch_shapes=[
            vm((slots, width), F32),
            vm((3, slots), F32),
            vm((3, kb), F32),
            vm((kb, width), F32),
            vm((width, width), F32),
            vm((width, width), F32),
            vm((width, width), F32),
            vm((width, width), F32),
            vm((slots, width), F32),
            vm((8, slots), F32),
            vm((8, kbpad), F32),
            vm((2, slots, hw), F32),
            vm((2, plane, slots, hw), F32),
            vm((plane, 8, slots), F32),
            vm((nz, 8, kbpad), F32),
            vm((2, slots, width), F32),
            vm((2, 8, slots), F32),
            vm((kpad, 128), BF16),
            vm((kpad, natoms), BF16),
            vm((kpad, natoms), BF16),
            vm((kpad, natoms), BF16),
            vm((kpad, natoms), BF16),
            vm((2, natoms, width), BF16),
            vm((2, nz, 2, 2, half, hw), F32),
            vm((2, nz, 2, half, hw), F32),
            vm((2, nz, 2, half, hw), F32),
            vm((2, 2, nz, 2, half, hw), F32),
            vm((2, 2, kpad, hw), F32),
            vm((2, 2, hw, kpad), BF16),
            vm((2, 2, hw, kpad), BF16),
            vm((2, plane, hw, slots), F32),
            vm((2, plane, hw, slots), F32),
            vm((slots, width), F32),
            dma((8,)),
            dma((plane,)),
            dma((plane,)),
            dma((2, plane)),
            dma((2, plane)),
            dma((2, 2)),
            dma((2, 2)),
            dma((nz,)),
            dma((nz,)),
            dma((2, nz)),
            dma((2, nz)),
            dma((2, nz, 2)),
            dma((2, 2, nz, 2)),
            dma((2, 2, 2, nz)),
            dma((2, 2, nz, 2)),
            dma((2, 2, nz)),
            dma((2, plane)),
            dma((2, plane)),
        ],
        compiler_params=pltpu.CompilerParams(collective_id=0, has_side_effects=True),
        name="ewald_layer",
    )(cell_counts, neighbours, nbr_count, feats, positions, kvec, filters, w_msg, w_val, w_one, w_two)


def solution(mesh):
    nz = 4 if mesh.shape["waves"] % 4 == 0 else 2
    placed = (
        P(("rows", "waves"), None),
        P(None, ("rows", "waves")),
        P(("rows", "waves")),
        P(("rows", "waves"), None),
        P(("rows", "waves")),
        P(None, "waves"),
        P("waves", None),
        P(),
        P(),
        P(),
        P(),
    )
    return jax.shard_map(
        functools.partial(shards, nz),
        mesh=mesh,
        in_specs=placed,
        out_specs=P(("rows", "waves"), None),
        check_vma=False,
    )
```

```python
import functools
import math

import jax
import jax.numpy as jnp
from jax import lax
from jax.experimental import pallas as pl
from jax.experimental.pallas import tpu as pltpu
from jax.sharding import PartitionSpec as P

MESH = pl.DeviceIdType.MESH
F32 = jnp.float32
BF16 = jnp.bfloat16

SIN = (4.44286798, -7.30744541, 3.5948021, -0.78440363)
COS = (1.4142135, -6.97885099, 5.73946117, -1.88356299, 0.31069819)


def split(x):
    high = x.astype(BF16)
    return high, (x - high.astype(F32)).astype(BF16)


def split3(x):
    a = x.astype(BF16).astype(F32)
    rest = x - a
    b = rest.astype(BF16).astype(F32)
    return a, b, rest - b


def mm(a, b):
    return jnp.dot(a, b, preferred_element_type=F32)


def dot3(a, b):
    return mm(a[0], b[0]) + mm(a[0], b[1]) + mm(a[1], b[0])


def horner(y, coefficients):
    total = y * coefficients[-1] + coefficients[-2]
    for coefficient in coefficients[-3::-1]:
        total = total * y + coefficient
    return total


def sincos(turns):
    x = turns - jnp.round(turns)
    y = x * x
    s = x * horner(y, SIN)
    c = horner(y, COS)
    return s * c, 1.0 - s * s


def columns(rows):
    height, width = rows.shape
    return jnp.concatenate([rows, jnp.zeros((128 - height, width), F32)], axis=0).T


def body(
    nz, plane, scale,
    counts_in, neigh_in, ncount_in, feats_in, pos_in, kv_in, filt_in, w_msg_in, w_val_in, w_one_in, w_two_in,
    out,
    counts, neigh, ncount, feats, pos3, kv3, filt, w_msg, w_val, w_one, w_two,
    fm, pos, kv, vals, vals_all, pos_all, kv_all, near_feat, near_pos, via_feat, via_pos, km, ch, cl, sh, sl, fcat,
    s_acc, xbuf, zs, zr, f_all, ft, es, er, msg, filt_far,
    s_in, s_pos, r_pos, s_val, r_val, s_near, r_near, s_via, r_via, s_on, s_kv, r_kv, s_x, r_x, s_z, r_z, s_f, r_f, s_g, s_e, r_e, s_filt, r_filt,
):
    slots, width = feats.shape
    kb = filt.shape[0]
    half = kb // 2
    hw = width // 2
    qw = hw // 2
    pieces = 4
    kall = nz * kb
    kpad = km.shape[0]
    cells = counts.shape[0]
    cell = slots // cells
    waves = nz * plane
    r = lax.axis_index("rows")
    w = lax.axis_index("waves")
    z = w // plane
    p = w % plane
    other = (1 - r, w)
    place = r * waves + w
    devices = 2 * waves
    scope = jax.named_scope
    at_low = p == 0
    at_high = p == plane - 1
    at_edge = at_low | at_high
    facing = z * plane + plane - 1 - p
    met = at_edge & ((z == 0) | (z == nz - 1))

    def plane_dev(j):
        return (r, z * plane + (p + j) % plane)

    def z_dev(j):
        return (r, ((z + j) % nz) * plane + p)

    def rcopy(src, dst, ssem, rsem, dev):
        return pltpu.make_async_remote_copy(
            src_ref=src, dst_ref=dst, send_sem=ssem, recv_sem=rsem, device_id=dev, device_id_type=MESH
        )

    def rows_of(block):
        return pl.ds(pl.multiple_of(block * slots, slots), slots)

    loads = [
        pltpu.make_async_copy(src, dst, s_in.at[i])
        for i, (src, dst) in enumerate(
            (
                (pos_in, pos3),
                (kv_in, kv3),
                (feats_in, feats),
                (w_val_in, w_val),
                (filt_in, filt),
                (w_msg_in, w_msg),
                (w_one_in, w_one),
                (w_two_in, w_two),
                (counts_in, counts),
                (neigh_in, neigh),
                (ncount_in, ncount),
            )
        )
    ]
    for load in loads:
        load.start()

    natoms = plane * slots
    lower = z < nz // 2
    rank = jnp.where(lower, z, nz - 1 - z)
    side_z = nz // 2
    inner = rank == side_z - 1
    outer = jnp.logical_not(inner)
    sign = jnp.where(lower, 1, -1)
    toward = (r, (z + sign) * plane + p)
    away = (r, (z - sign) * plane + p)

    def block_at(j):
        block = nz - 1 - j if j < side_z else j - side_z
        return jnp.where(lower, block, nz - 1 - block)

    mine = pl.multiple_of(r * half, 8)

    barrier = pltpu.get_barrier_semaphore()
    pl.semaphore_signal(barrier, inc=1, device_id=other, device_id_type=MESH)

    @pl.when(met)
    def _():
        pl.semaphore_signal(barrier, inc=1, device_id=(1 - r, facing), device_id_type=MESH)

    for j in range(1, nz):
        pl.semaphore_signal(barrier, inc=1, device_id=z_dev(j), device_id_type=MESH)

    @pl.loop(1, plane)
    def _(j):
        pl.semaphore_signal(barrier, inc=1, device_id=plane_dev(j), device_id_type=MESH)

    with scope("A_load"):
        loads[0].wait()
        loads[1].wait()
        pos[...] = jnp.zeros_like(pos)
        pos[0:3, :] = pos3[...]
        kv[...] = jnp.zeros_like(kv)
        kv[0:3, 0:kb] = kv3[...] * (0.5 / math.pi)
        loads[2].wait()
        for load in loads[8:]:
            load.wait()
        slot_ids = lax.broadcasted_iota(jnp.int32, (cell, width), 0)
        for c in range(cells):
            part = slice(c * cell, (c + 1) * cell)
            fm[part, :] = jnp.where(slot_ids < counts[c], feats[part, :], 0.0)
        loads[3].wait()
        projected = dot3(split(fm[...]), split(w_val[...]))
        for h in range(2):
            vals[h] = projected[:, h * hw : (h + 1) * hw]

    loads[4].wait()
    with scope("A_barrier"):
        pl.semaphore_wait(barrier, nz + plane - 1 + jnp.where(met, 1, 0))

    def kv_copy(j):
        return rcopy(kv, kv_all.at[z], s_kv.at[j], r_kv.at[z], z_dev(j))

    def kv_arrival(j):
        q = (z + j) % nz
        return rcopy(kv, kv_all.at[q], s_kv.at[j], r_kv.at[q], z_dev(j))

    def pos_copy(j):
        return rcopy(pos, pos_all.at[p], s_pos.at[j], r_pos.at[p], plane_dev(j))

    def pos_arrival(q):
        return rcopy(pos, pos_all.at[q], s_pos.at[0], r_pos.at[q], other)

    def val_copy(h, j):
        return rcopy(vals.at[h], vals_all.at[h, p], s_val.at[h, j], r_val.at[h, p], plane_dev(j))

    def val_arrival(h, q):
        return rcopy(vals.at[h], vals_all.at[h, q], s_val.at[h, 0], r_val.at[h, q], other)

    def pair(feat_src, pos_src, feat_dst, pos_dst, ssem, rsem, dev):
        return (
            rcopy(pos_src, pos_dst, ssem.at[0], rsem.at[0], dev),
            rcopy(feat_src, feat_dst, ssem.at[1], rsem.at[1], dev),
        )

    def near_copies(side):
        dev = plane_dev(1 if side == 0 else plane - 1)
        return pair(fm, pos, near_feat.at[side], near_pos.at[side], s_near.at[side], r_near.at[side], dev)

    def via_copies():
        dev = (r, ((z + jnp.where(at_high, 1, nz - 1)) % nz) * plane + p)
        return pair(fm, pos, via_feat, via_pos, s_via, r_via, dev)

    def on_copies():
        side = jnp.where(at_high, 0, 1)
        flip = (at_high & (z == 0)) | (at_low & (z == nz - 1))
        dev = (jnp.where(flip, 1 - r, r), facing)
        return pair(via_feat, via_pos, near_feat.at[side], near_pos.at[side], s_on, r_near.at[side], dev)

    def start_near():
        for side, there in ((0, jnp.logical_not(at_high)), (1, jnp.logical_not(at_low))):

            @pl.when(there)
            def _():
                for copy in near_copies(side):
                    copy.start()

        @pl.when(at_edge)
        def _():
            for arrived, copy in zip(via_copies(), on_copies()):
                arrived.wait_recv()
                copy.start()

    def filt_copy():
        return rcopy(filt.at[pl.ds(mine, half), :], filt_far, s_filt.at[0], r_filt.at[0], toward)

    for j in range(1, nz):
        kv_copy(j).start()

    if nz > 2:

        @pl.when(outer)
        def _():
            filt_copy().start()

    @pl.loop(1, plane)
    def _(j):
        pos_copy(j).start()

    @pl.loop(1, plane)
    def _(j):
        val_copy(0, j).start()

    def place_k(block, rows):
        a, b, c = split3(rows)
        stack = [a, a, a, b, b, b, c, c, c]
        stack.append(jnp.zeros((128 - 8 * len(stack), rows.shape[1]), F32))
        km[pl.ds(pl.multiple_of(block * kb, 16), kb), :] = jnp.concatenate(stack, axis=0).T[:kb].astype(BF16)

    def place_v(h, q, block):
        a, b = split(block)
        fcat[h, rows_of(q), 0:hw] = a
        fcat[h, rows_of(q), hw:width] = b

    if kpad > kall:
        f_all[:, kall:, :] = jnp.zeros((pieces, kpad - kall, hw), F32)
    for h in range(2):
        place_v(h, p, vals[h])
    with scope("B_kv"):
        place_k(z, kv[...])
        if kpad > kall:
            km[kall:, :] = jnp.zeros((kpad - kall, 128), BF16)
        for j in [1, nz - 1] + list(range(2, nz - 1)) if nz > 2 else [1]:
            kv_arrival(j).wait_recv()
            if j == nz - 1:

                @pl.when(at_edge)
                def _():
                    for copy in via_copies():
                        copy.start()

            q = (z + j) % nz
            place_k(q, kv_all[q])

    def phases(q, rows3):
        stack = list(split3(rows3)) * 3
        stack.append(jnp.zeros((128 - 8 * len(stack), slots), F32))
        s, c = sincos(mm(km[...], jnp.concatenate(stack, axis=0).astype(BF16)))
        lanes = rows_of(q)
        a, b = split(c)
        ch[:, lanes] = a
        cl[:, lanes] = b
        a, b = split(s)
        sh[:, lanes] = a
        sl[:, lanes] = b

    pos_all[p] = pos[...]

    with scope("C_phases"):

        @pl.loop(0, plane)
        def _(j):
            q = (p + j) % plane

            @pl.when(j > 0)
            def _():
                with scope("c_poswait"):
                    pos_arrival(q).wait_recv()

            with scope("c_phase"):
                phases(q, pos_all[q])

            @pl.when(j == plane // 2)
            def _():
                @pl.loop(1, plane)
                def _(k):
                    val_copy(0, k).wait_send()

                @pl.loop(1, plane)
                def _(k):
                    val_copy(1, k).start()

    def partial_sums(h, j):
        zb = block_at(j)
        ks = pl.ds(pl.multiple_of(zb * kb, 16), kb)
        totals = []
        for hi, lo in ((ch, cl), (sh, sl)):
            wide = mm(hi[ks, :], fcat[h])
            totals.append(wide[:, :hw] + wide[:, hw:] + mm(lo[ks, :], fcat[h, :, 0:hw]))
        for i in range(2):
            piece = jnp.concatenate([total[:, i * qw : (i + 1) * qw] for total in totals], axis=1)
            for c in range(2):
                s_acc[h, zb, c, i] = piece[c * half : (c + 1) * half]

    def x_copy(h, j):
        zb = block_at(j)
        return rcopy(s_acc.at[h, zb, 1 - r], xbuf.at[h, zb], s_x.at[h, zb], r_x.at[h, zb], other)

    def s_hop(u, j, source):
        zb = block_at(j)
        return rcopy(zs.at[u, zb], zr.at[source, u, zb], s_z.at[u, zb], r_z.at[source, u, zb], toward)

    def gathered_sum(u, j, sources):
        zb = block_at(j)
        if u % 2 == 0:
            x_copy(u // 2, j).wait_recv()
        total = s_acc[u // 2, zb, r, u % 2] + xbuf[u // 2, zb, u % 2]
        for source in sources:
            s_hop(u, j, source).wait_recv()
            total = total + zr[source, u, zb]
        return total

    def send_sum(u, j, is_inner):
        zs[u, block_at(j)] = gathered_sum(u, j, (0,) if is_inner and nz > 2 else ())
        s_hop(u, j, 1 if is_inner else 0).start()

    def share(u, zb, c):
        return f_all.at[u, pl.ds(pl.multiple_of((zb * 2 + c) * half, 8), half), :]

    def f_hop(u, zb, way, dev):
        here = share(u, zb, r)
        return rcopy(here, here, s_f.at[u, zb, way], r_f.at[u, zb, r], dev)

    def f_relay(u, zb):
        here = share(u, zb, r)
        return rcopy(here, here, s_g.at[u, zb], r_f.at[u, zb, r], other)

    def f_arrival(u, zb, c):
        here = share(u, zb, c)
        return rcopy(here, here, s_g.at[u, zb], r_f.at[u, zb, c], other)

    def finish_sum(u, j):
        zb = block_at(j)
        lanes = slice(u * qw, (u + 1) * qw)
        rows = filt[pl.ds(mine, half), lanes] if j == nz - 1 else filt_far[:, lanes]
        rows = jnp.concatenate([rows, rows], axis=1) * scale
        total = gathered_sum(u, j, (0, 1) if nz > 2 else (1,))
        f_all[u, pl.ds(pl.multiple_of((zb * 2 + r) * half, 8), half), :] = rows * total
        if nz > 2:
            f_hop(u, zb, 1, away).start()
        f_hop(u, zb, 0, toward).start()
        f_relay(u, zb).start()

    def take_filtered(u, j, is_inner):
        zb = block_at(j)
        f_arrival(u, zb, r).wait_recv()
        if is_inner and nz > 2:
            f_hop(u, zb, 1, away).start()
        f_relay(u, zb).start()

    def back(u, j):
        lanes = rows_of((p + j) % plane)
        total = jnp.zeros((qw, slots), F32)
        for part, (hi, lo) in enumerate(((ch, cl), (sh, sl))):
            both = mm(ft[u, part], hi[:, lanes])
            total = total + both[:qw] + both[qw:] + mm(ft[u, part, 0:qw, :], lo[:, lanes])
        es[u, j] = total

    def e_copy(u, j):
        return rcopy(es.at[u, j], er.at[u, j], s_e.at[u, j], r_e.at[u, j], plane_dev(j))

    def gather(u):
        for zb in range(nz):
            f_arrival(u, zb, 1 - r).wait_recv()
        a, b = split(f_all[u].T)
        for part in range(2):
            rows = slice(part * qw, (part + 1) * qw)
            ft[u, part, 0:qw, :] = a[rows]
            ft[u, part, qw:hw, :] = b[rows]

    def back_range(u, start, stop):
        @pl.loop(start, stop)
        def _(j):
            back(u, j)
            e_copy(u, j).start()

    def take_vals(h):
        @pl.loop(1, plane)
        def _(j):
            q = (p + j) % plane
            val_arrival(h, q).wait_recv()
            place_v(h, q, vals_all[h, q])

    def own_message():
        first = place * cells
        total_cells = cells * devices
        own_cols = columns(pos[...])
        same = lax.broadcasted_iota(jnp.int32, (slots, slots), 0) == lax.broadcasted_iota(
            jnp.int32, (slots, slots), 1
        )
        row_cell = lax.broadcasted_iota(jnp.int32, (slots, slots), 0) // cell
        col_cell = lax.broadcasted_iota(jnp.int32, (slots, slots), 1) // cell

        def listed(c, target):
            found = jnp.float32(0.0)
            for b in range(neigh.shape[1]):
                hit = (neigh[c, b] == target) & (b < ncount[c])
                found = found + jnp.where(hit, 1.0, 0.0)
            return found

        gathered = jnp.zeros((slots, width), F32)
        for shift in (-1, 0, 1):
            if shift:
                for copy in near_copies(0 if shift < 0 else 1):
                    copy.wait_recv()
            near = pos[...] if shift == 0 else near_pos[0 if shift < 0 else 1]
            atoms = fm[...] if shift == 0 else near_feat[0 if shift < 0 else 1]
            dist = jnp.zeros((slots, slots), F32)
            for axis in range(3):
                diff = own_cols[:, axis : axis + 1] - near[axis : axis + 1]
                dist = dist + diff * diff
            live = jnp.zeros((slots, slots), F32)
            for c in range(cells):
                for t in range(cells):
                    target = (first + shift * cells + t + total_cells) % total_cells
                    live = jnp.where((row_cell == c) & (col_cell == t), listed(c, target), live)
            weight = jnp.exp(-0.125 * dist) * live
            if shift == 0:
                weight = jnp.where(same, 0.0, weight)
            gathered = gathered + dot3(split(weight), split(atoms))
        msg[...] = feats[...] + 0.125 * dot3(split(gathered), split(w_msg[...]))

    with scope("D_takeA"):
        take_vals(0)
    def at_inner(steps):
        @pl.when(inner)
        def _():
            for step, u, j in steps:
                step(u, j, True) if step is not finish_sum else step(u, j)

    def at_outer(steps):
        if nz > 2:

            @pl.when(outer)
            def _():
                for step, u, j in steps:
                    step(u, j, False)

    def sums(h):
        for j in range(nz):
            partial_sums(h, j)
            x_copy(h, j).start()
            if j > 1:
                at_outer([(send_sum, 2 * h, j - 2)])
        at_outer([(send_sum, 2 * h, j) for j in range(max(nz - 2, 0), nz)])
        at_outer([(send_sum, 2 * h + 1, j) for j in range(nz)])

    S, F, T = send_sum, finish_sum, take_filtered
    rest = list(range(1, side_z))

    def early(step, u):
        return [(step, u, 0 if step is not finish_sum else side_z)]

    def late(step, u):
        return [(step, u, j if step is not finish_sum else side_z + j) for j in rest]

    def own(u):
        return [(T, u, side_z)]

    def own_late(u):
        return [(T, u, side_z + j) for j in rest]

    cut = 1 + (plane - 1) // 3, 1 + 2 * (plane - 1) // 3

    with scope("D_psumA"):
        sums(0)
    with scope("D_send0"):
        at_inner(early(S, 0) + late(S, 0))
    start_near()
    with scope("E_takeB"):
        take_vals(1)
    with scope("E_psumB"):
        sums(1)
    with scope("F_mid"):
        if nz > 2:

            @pl.when(inner)
            def _():
                filt_copy().wait_recv()

        at_inner(
            early(F, 0) + early(S, 1) + late(F, 0) + late(S, 1) + early(T, 0) + early(F, 1) + late(T, 0)
            + early(S, 2) + late(F, 1) + late(S, 2)
        )
        at_outer(own(0) + own_late(0) + early(T, 0) + own(1) + late(T, 0))
    for load in loads[5:8]:
        load.wait()
    if nz > 2:
        with scope("F_msg"):

            @pl.when(outer)
            def _():
                own_message()

    with scope("G_gather0"):
        gather(0)
    with scope("G_back0"):
        back_range(0, 1, cut[1])
    with scope("G_a"):
        at_inner(early(T, 1) + early(F, 2) + late(T, 1) + early(S, 3) + late(F, 2) + late(S, 3))
        at_outer(own_late(1))
    with scope("G_back0"):
        back_range(0, cut[1], plane)
    with scope("G_b"):
        at_outer(early(T, 1) + own(2) + late(T, 1))
    with scope("G_gather1"):
        gather(1)
    with scope("G_back1"):
        back_range(1, 1, cut[0])
    with scope("G_c"):
        at_inner(early(T, 2) + early(F, 3) + late(T, 2) + late(F, 3))
        at_outer(own_late(2))
    with scope("G_back1"):
        back_range(1, cut[0], plane)
    with scope("G_d"):
        at_outer(early(T, 2) + own(3) + late(T, 2))
    with scope("G_gather2"):
        gather(2)
    with scope("G_back2"):
        back_range(2, 1, cut[0])
    with scope("G_e"):
        at_inner(early(T, 3))
    with scope("G_back2"):
        back_range(2, cut[0], cut[1])
    with scope("G_f"):
        at_inner(late(T, 3))
    with scope("G_back2"):
        back_range(2, cut[1], plane)
    with scope("K_take"):
        at_outer(own_late(3) + early(T, 3) + late(T, 3))
    with scope("K_msg"):

        @pl.when(inner)
        def _():
            own_message()

    with scope("K_gather3"):
        gather(3)
    with scope("K_back3"):
        back_range(3, 1, plane)
    with scope("K_own"):
        for u in range(pieces):
            back(u, 0)

    with scope("M_ewait"):
        for u in range(pieces):

            @pl.loop(1, plane)
            def _(j):
                e_copy(u, j).wait_recv()
                es[u, 0] = es[u, 0] + er[u, j]

    with scope("N_mlp"):
        summed = msg[...] + jnp.concatenate([es[u, 0] for u in range(pieces)], axis=0).T
        normed = summed / jnp.sqrt(jnp.mean(summed * summed, axis=1, keepdims=True) + 1e-06)
        v = dot3(split(normed), split(w_one[...]))
        hidden = v / (1.0 + jnp.exp(-v))
        result = summed + dot3(split(hidden), split(w_two[...]))
        for c in range(cells):
            part = slice(c * cell, (c + 1) * cell)
            out[part, :] = jnp.where(slot_ids < counts[c], result[part], 0.0)

    _sc = scope("O_waits")
    _sc.__enter__()
    for j in range(1, nz):
        kv_copy(j).wait_send()
    for j in range(nz):
        for h in range(2):
            x_copy(h, j).wait_send()
        for u in range(pieces):
            zb = block_at(j)
            f_relay(u, zb).wait_send()
            if j < side_z:
                s_hop(u, j, 0).wait_send()
            elif nz > 2:

                @pl.when(outer)
                def _():
                    s_hop(u, j, 0).wait_send()

            @pl.when(inner)
            def _():
                if nz > 2:
                    f_hop(u, zb, 1, away).wait_send()
                if j >= side_z:
                    f_hop(u, zb, 0, toward).wait_send()

    if nz > 2:

        @pl.when(outer)
        def _():
            filt_copy().wait_send()

    @pl.loop(1, plane)
    def _(j):
        pos_copy(j).wait_send()
        val_copy(1, j).wait_send()
        for u in range(pieces):
            e_copy(u, j).wait_send()

    for side, there in ((0, jnp.logical_not(at_high)), (1, jnp.logical_not(at_low))):

        @pl.when(there)
        def _():
            for copy in near_copies(side):
                copy.wait_send()

    @pl.when(at_edge)
    def _():
        for copy in via_copies() + on_copies():
            copy.wait_send()

    _sc.__exit__(None, None, None)


def shards(
    nz, feats, positions, cell_counts, neighbours, nbr_count, kvec, filters, w_msg, w_val, w_one, w_two
):
    slots, width = feats.shape
    kb = kvec.shape[1]
    waves = lax.axis_size("waves")
    plane = waves // nz
    devices = lax.axis_size("rows") * waves
    kpad = -(-nz * kb // 128) * 128
    kbpad = -(-kb // 128) * 128
    half = kb // 2
    hw = width // 2
    scale = 1.0 / math.sqrt(float(slots * devices) * float(kb * waves))
    natoms = plane * slots
    vm = pltpu.VMEM
    dma = pltpu.SemaphoreType.DMA
    any_spec = pl.BlockSpec(memory_space=pl.ANY)
    vmem_spec = pl.BlockSpec(memory_space=pltpu.VMEM)
    return pl.pallas_call(
        functools.partial(body, nz, plane, scale),
        out_shape=pltpu.VMEM((slots, width), F32),
        in_specs=[any_spec] * 11,
        out_specs=vmem_spec,
        scratch_shapes=[
            pltpu.SMEM(cell_counts.shape, jnp.int32),
            pltpu.SMEM(neighbours.shape, jnp.int32),
            pltpu.SMEM(nbr_count.shape, jnp.int32),
            vm((slots, width), F32),
            vm((3, slots), F32),
            vm((3, kb), F32),
            vm((kb, width), F32),
            vm((width, width), F32),
            vm((width, width), F32),
            vm((width, width), F32),
            vm((width, width), F32),
            vm((slots, width), F32),
            vm((8, slots), F32),
            vm((8, kbpad), F32),
            vm((2, slots, hw), F32),
            vm((2, plane, slots, hw), F32),
            vm((plane, 8, slots), F32),
            vm((nz, 8, kbpad), F32),
            vm((2, slots, width), F32),
            vm((2, 8, slots), F32),
            vm((slots, width), F32),
            vm((8, slots), F32),
            vm((kpad, 128), BF16),
            vm((kpad, natoms), BF16),
            vm((kpad, natoms), BF16),
            vm((kpad, natoms), BF16),
            vm((kpad, natoms), BF16),
            vm((2, natoms, width), BF16),
            vm((2, nz, 2, 2, half, hw), F32),
            vm((2, nz, 2, half, hw), F32),
            vm((4, nz, half, hw), F32),
            vm((2, 4, nz, half, hw), F32),
            vm((4, kpad, hw), F32),
            vm((4, 2, hw, kpad), BF16),
            vm((4, plane, hw // 2, slots), F32),
            vm((4, plane, hw // 2, slots), F32),
            vm((slots, width), F32),
            vm((half, width), F32),
            dma((11,)),
            dma((plane,)),
            dma((plane,)),
            dma((2, plane)),
            dma((2, plane)),
            dma((2, 2)),
            dma((2, 2)),
            dma((2,)),
            dma((2,)),
            dma((2,)),
            dma((nz,)),
            dma((nz,)),
            dma((2, nz)),
            dma((2, nz)),
            dma((4, nz)),
            dma((2, 4, nz)),
            dma((4, nz, 2)),
            dma((4, nz, 2)),
            dma((4, nz)),
            dma((4, plane)),
            dma((4, plane)),
            dma((1,)),
            dma((1,)),
        ],
        compiler_params=pltpu.CompilerParams(collective_id=0, has_side_effects=True),
        name="ewald_layer",
    )(cell_counts, neighbours, nbr_count, feats, positions, kvec, filters, w_msg, w_val, w_one, w_two)


def solution(mesh):
    nz = 4 if mesh.shape["waves"] % 4 == 0 else 2
    placed = (
        P(("rows", "waves"), None),
        P(None, ("rows", "waves")),
        P(("rows", "waves")),
        P(("rows", "waves"), None),
        P(("rows", "waves")),
        P(None, "waves"),
        P("waves", None),
        P(),
        P(),
        P(),
        P(),
    )
    return jax.shard_map(
        functools.partial(shards, nz),
        mesh=mesh,
        in_specs=placed,
        out_specs=P(("rows", "waves"), None),
        check_vma=False,
    )
```

```python
import functools
import math

import jax
import jax.numpy as jnp
from jax import lax
from jax.experimental import pallas as pl
from jax.experimental.pallas import tpu as pltpu
from jax.sharding import PartitionSpec as P

MESH = pl.DeviceIdType.MESH
F32 = jnp.float32
BF16 = jnp.bfloat16

SIN = (4.44286798, -7.30744541, 3.5948021, -0.78440363)
COS = (1.4142135, -6.97885099, 5.73946117, -1.88356299, 0.31069819)


def split(x):
    high = x.astype(BF16)
    return high, (x - high.astype(F32)).astype(BF16)


def split3(x):
    a = x.astype(BF16).astype(F32)
    rest = x - a
    b = rest.astype(BF16).astype(F32)
    return a, b, rest - b


def mm(a, b):
    return jnp.dot(a, b, preferred_element_type=F32)


def dot3(a, b):
    return mm(a[0], b[0]) + mm(a[0], b[1]) + mm(a[1], b[0])


def horner(y, coefficients):
    total = y * coefficients[-1] + coefficients[-2]
    for coefficient in coefficients[-3::-1]:
        total = total * y + coefficient
    return total


def sincos(turns):
    x = turns - jnp.round(turns)
    y = x * x
    s = x * horner(y, SIN)
    c = horner(y, COS)
    return s * c, 1.0 - s * s


def columns(rows):
    height, width = rows.shape
    return jnp.concatenate([rows, jnp.zeros((128 - height, width), F32)], axis=0).T


def body(
    nz, plane, scale,
    counts_in, neigh_in, ncount_in, feats_in, pos_in, kv_in, filt_in, w_msg_in, w_val_in, w_one_in, w_two_in,
    out,
    counts, neigh, ncount, feats, pos3, kv3, filt, w_val, w_late,
    fm, pos, kv, vals, vals_all, pos_all, kv_all, near, via, km, ch, cl, sh, sl, fcat,
    s_acc, xbuf, zs, zr, f_all, ft, es, er, msg, filt_far,
    s_in, s_late, s_pos, r_pos, s_val, r_val, s_near, r_near, s_via, r_via, s_on, s_kv, r_kv, s_x, r_x, s_z, r_z, s_f, r_f, s_g, r_g, s_e, r_e, s_filt, r_filt,
):
    slots, width = feats.shape
    kb = filt.shape[0]
    half = kb // 2
    hw = width // 2
    qw = hw // 2
    pieces = 4
    kall = nz * kb
    kpad = km.shape[0]
    cells = counts.shape[0]
    cell = slots // cells
    waves = nz * plane
    r = lax.axis_index("rows")
    w = lax.axis_index("waves")
    z = w // plane
    p = w % plane
    other = (1 - r, w)
    place = r * waves + w
    devices = 2 * waves
    scope = jax.named_scope
    at_low = p == 0
    at_high = p == plane - 1
    at_edge = at_low | at_high
    facing = z * plane + plane - 1 - p
    met = at_edge & ((z == 0) | (z == nz - 1))

    def plane_dev(j):
        return (r, z * plane + (p + j) % plane)

    bits = (plane - 1).bit_length()

    def peer(j):
        q = p
        for b in range(bits):
            q = q + ((j // (1 << b)) % 2) * (1 << b) * (1 - 2 * ((p // (1 << b)) % 2))
        return q

    def peer_dev(j):
        return (r, z * plane + peer(j))

    def z_dev(j):
        return (r, ((z + j) % nz) * plane + p)

    def rcopy(src, dst, ssem, rsem, dev):
        return pltpu.make_async_remote_copy(
            src_ref=src, dst_ref=dst, send_sem=ssem, recv_sem=rsem, device_id=dev, device_id_type=MESH
        )

    def rows_of(block):
        return pl.ds(pl.multiple_of(block * slots, slots), slots)

    loads = [
        pltpu.make_async_copy(src, dst, s_in.at[i])
        for i, (src, dst) in enumerate(
            (
                (pos_in, pos3),
                (kv_in, kv3),
                (feats_in, feats),
                (w_val_in, w_val),
                (filt_in, filt),
                (counts_in, counts),
                (neigh_in, neigh),
                (ncount_in, ncount),
            )
        )
    ]
    late_loads = [
        pltpu.make_async_copy(src, w_late.at[i], s_late) for i, src in enumerate((w_msg_in, w_one_in, w_two_in))
    ]
    for load in loads + late_loads:
        load.start()

    natoms = plane * slots
    lower = z < nz // 2
    rank = jnp.where(lower, z, nz - 1 - z)
    side_z = nz // 2
    inner = rank == side_z - 1
    outer = jnp.logical_not(inner)
    sign = jnp.where(lower, 1, -1)
    toward = (r, (z + sign) * plane + p)
    away = (r, (z - sign) * plane + p)

    def block_at(j):
        block = nz - 1 - j if j < side_z else j - side_z
        return jnp.where(lower, block, nz - 1 - block)

    mine = pl.multiple_of(r * half, 8)

    barrier = pltpu.get_barrier_semaphore()
    pl.semaphore_signal(barrier, inc=1, device_id=other, device_id_type=MESH)

    @pl.when(met)
    def _():
        pl.semaphore_signal(barrier, inc=1, device_id=(1 - r, facing), device_id_type=MESH)

    for j in range(1, nz):
        pl.semaphore_signal(barrier, inc=1, device_id=z_dev(j), device_id_type=MESH)

    @pl.loop(1, plane)
    def _(j):
        pl.semaphore_signal(barrier, inc=1, device_id=plane_dev(j), device_id_type=MESH)

    with scope("A_load"):
        loads[0].wait()
        loads[1].wait()
        pos[...] = jnp.zeros_like(pos)
        pos[0:3, :] = pos3[...]
        kv[...] = jnp.zeros_like(kv)
        kv[0:3, 0:kb] = kv3[...] * (0.5 / math.pi)
    with scope("A_barrier"):
        pl.semaphore_wait(barrier, nz + plane - 1 + jnp.where(met, 1, 0))

    def kv_copy(j):
        return rcopy(kv, kv_all.at[z], s_kv, r_kv.at[z], z_dev(j))

    def kv_arrival(j):
        q = (z + j) % nz
        return rcopy(kv, kv_all.at[q], s_kv, r_kv.at[q], z_dev(j))

    def pos_copy(j):
        return rcopy(pos, pos_all.at[p], s_pos, r_pos, peer_dev(j))

    def val_copy(h, j):
        return rcopy(vals.at[h], vals_all.at[h, p], s_val.at[h], r_val.at[h], peer_dev(j))

    def all_pos():
        block = pos_all.at[pl.ds(0, plane - 1)]
        return rcopy(block, block, s_pos, r_pos, other)

    def all_vals(h):
        block = vals_all.at[h, pl.ds(0, plane - 1)]
        return rcopy(block, block, s_val.at[h], r_val.at[h], other)

    def near_copy(side):
        dev = plane_dev(1 if side == 0 else plane - 1)
        return rcopy(fm, near.at[side], s_near.at[side], r_near.at[side], dev)

    def via_copy():
        dev = (r, ((z + jnp.where(at_high, 1, nz - 1)) % nz) * plane + p)
        return rcopy(fm, via, s_via, r_via, dev)

    def on_copy():
        side = jnp.where(at_high, 0, 1)
        flip = (at_high & (z == 0)) | (at_low & (z == nz - 1))
        dev = (jnp.where(flip, 1 - r, r), facing)
        return rcopy(via, near.at[side], s_on, r_near.at[side], dev)

    def start_near():
        for side, there in ((0, jnp.logical_not(at_high)), (1, jnp.logical_not(at_low))):

            @pl.when(there)
            def _():
                near_copy(side).start()

    def start_on():
        @pl.when(at_edge)
        def _():
            via_copy().wait_recv()
            on_copy().start()

    def filt_copy():
        return rcopy(filt.at[pl.ds(mine, half), :], filt_far, s_filt.at[0], r_filt.at[0], toward)

    for j in range(1, nz):
        kv_copy(j).start()

    @pl.loop(1, plane)
    def _(j):
        pos_copy(j).start()

    slot_ids = lax.broadcasted_iota(jnp.int32, (cell, width), 0)
    with scope("B_project"):
        loads[2].wait()
        for load in loads[5:]:
            load.wait()
        for c in range(cells):
            part = slice(c * cell, (c + 1) * cell)
            fm[part, :] = jnp.where(slot_ids < counts[c], feats[part, :], 0.0)
        fm[slots:, 0:slots] = pos[...]
        loads[3].wait()
        projected = dot3(split(fm[0:slots, :]), split(w_val[...]))
        for h in range(2):
            vals[h] = projected[:, h * hw : (h + 1) * hw]

    @pl.loop(1, plane)
    def _(j):
        val_copy(0, plane - j).start()

    loads[4].wait()
    if nz > 2:

        @pl.when(outer)
        def _():
            filt_copy().start()

    def place_k(block, rows):
        a, b, c = split3(rows)
        stack = [a, a, a, b, b, b, c, c, c]
        stack.append(jnp.zeros((128 - 8 * len(stack), rows.shape[1]), F32))
        km[pl.ds(pl.multiple_of(block * kb, 16), kb), :] = jnp.concatenate(stack, axis=0).T[:kb].astype(BF16)

    def place_v(h, q, block):
        a, b = split(block)
        fcat[h, rows_of(q), 0:hw] = a
        fcat[h, rows_of(q), hw:width] = b

    if kpad > kall:
        f_all[:, kall:, :] = jnp.zeros((pieces, kpad - kall, hw), F32)
    for h in range(2):
        place_v(h, p, vals[h])
    with scope("B_kv"):
        place_k(z, kv[...])
        if kpad > kall:
            km[kall:, :] = jnp.zeros((kpad - kall, 128), BF16)
        for j in [1, nz - 1] + list(range(2, nz - 1)) if nz > 2 else [1]:
            kv_arrival(j).wait_recv()
            if j == nz - 1:

                @pl.when(at_edge)
                def _():
                    via_copy().start()

            q = (z + j) % nz
            place_k(q, kv_all[q])

    def phases(q, rows3):
        stack = list(split3(rows3)) * 3
        stack.append(jnp.zeros((128 - 8 * len(stack), slots), F32))
        s, c = sincos(mm(km[...], jnp.concatenate(stack, axis=0).astype(BF16)))
        lanes = rows_of(q)
        a, b = split(c)
        ch[:, lanes] = a
        cl[:, lanes] = b
        a, b = split(s)
        sh[:, lanes] = a
        sl[:, lanes] = b

    pos_all[p] = pos[...]

    with scope("C_phases"):

        @pl.loop(0, plane)
        def _(j):
            q = peer(j)

            @pl.when(j == 1)
            def _():
                with scope("c_poswait"):
                    all_pos().wait_recv()

            with scope("c_phase"):
                phases(q, pos_all[q])

            @pl.when(j == plane // 2)
            def _():
                all_vals(0).wait_send()

                @pl.loop(1, plane)
                def _(k):
                    val_copy(1, plane - k).start()


    def partial_sums(h, j):
        zb = block_at(j)
        ks = pl.ds(pl.multiple_of(zb * kb, 16), kb)
        totals = []
        for hi, lo in ((ch, cl), (sh, sl)):
            wide = mm(hi[ks, :], fcat[h])
            totals.append(wide[:, :hw] + wide[:, hw:] + mm(lo[ks, :], fcat[h, :, 0:hw]))
        for i in range(2):
            piece = jnp.concatenate([total[:, i * qw : (i + 1) * qw] for total in totals], axis=1)
            for c in range(2):
                s_acc[h, zb, c, i] = piece[c * half : (c + 1) * half]

    def x_copy(h, j):
        zb = block_at(j)
        return rcopy(s_acc.at[h, zb, 1 - r], xbuf.at[h, zb], s_x, r_x.at[h, zb], other)

    def units(u):
        if u < pieces - 1 or half % 16:
            return [(u, slice(0, half))]
        return [(u, slice(0, half // 2)), (u + 1, slice(half // 2, half))]

    def s_hop(u, j, source, unit):
        zb = block_at(j)
        index, rows = unit
        return rcopy(zs.at[u, zb, rows], zr.at[source, u, zb, rows], s_z, r_f.at[index, zb] if source else r_z.at[index, zb], toward)

    def gathered_sum(u, j, sources, unit):
        zb = block_at(j)
        rows = unit[1]
        total = s_acc[u // 2, zb, r, u % 2, rows, :] + xbuf[u // 2, zb, u % 2, rows, :]
        for source in sources:
            s_hop(u, j, source, unit).wait_recv()
            total = total + zr[source, u, zb, rows, :]
        return total

    def send_sum(u, j, is_inner):
        if u % 2 == 0:
            x_copy(u // 2, j).wait_recv()
        for unit in units(u):
            zs[u, block_at(j), unit[1], :] = gathered_sum(u, j, (0,) if is_inner and nz > 2 else (), unit)
            s_hop(u, j, 1 if is_inner else 0, unit).start()

    def share(u, zb, rows):
        start = pl.multiple_of((zb * 2 + r) * half + rows.start, 8)
        return f_all.at[u, pl.ds(start, rows.stop - rows.start), :]

    def f_hop(u, zb, way, dev, unit):
        here = share(u, zb, unit[1])
        return rcopy(here, here, s_f.at[way], r_f.at[unit[0], zb], dev)

    def f_relay(u, zb, unit):
        here = share(u, zb, unit[1])
        return rcopy(here, here, s_g, r_g.at[u], other)

    def filtered_bytes(pieces_sent, ssem, rsem):
        block = f_all.at[pl.ds(0, pieces_sent), pl.ds(0, nz * half)]
        return rcopy(block, block, ssem, rsem, other)

    def finish_sum(u, j):
        zb = block_at(j)
        lanes = slice(u * qw, (u + 1) * qw)
        kept = filt[pl.ds(mine, half), lanes] if j == nz - 1 else filt_far[:, lanes]
        kept = jnp.concatenate([kept, kept], axis=1) * scale
        if u % 2 == 0:
            x_copy(u // 2, j).wait_recv()
        for unit in units(u):
            rows = unit[1]
            total = gathered_sum(u, j, (0, 1) if nz > 2 else (1,), unit)
            start = pl.multiple_of((zb * 2 + r) * half + rows.start, 8)
            f_all[u, pl.ds(start, rows.stop - rows.start), :] = kept[rows] * total
            f_hop(u, zb, 0, toward, unit).start()
            if nz > 2:
                f_hop(u, zb, 1, away, unit).start()
            f_relay(u, zb, unit).start()

    def take_filtered(u, j, is_inner):
        zb = block_at(j)
        for unit in units(u):
            f_hop(u, zb, 0, other, unit).wait_recv()
            if is_inner and nz > 2:
                f_hop(u, zb, 1, away, unit).start()
            f_relay(u, zb, unit).start()

    def back(u, j):
        lanes = rows_of(peer(j))
        total = jnp.zeros((qw, slots), F32)
        for part, (hi, lo) in enumerate(((ch, cl), (sh, sl))):
            both = mm(ft[u, part], hi[:, lanes])
            total = total + both[:qw] + both[qw:] + mm(ft[u, part, 0:qw, :], lo[:, lanes])
        es[u, j] = total

    def e_copy(u, j):
        return rcopy(es.at[u, j], er.at[u, j], s_e, r_e.at[u // (pieces - 1)], peer_dev(j))

    def all_e(start, stop, group):
        block = er.at[pl.ds(start, stop - start), pl.ds(1, plane - 1)]
        return rcopy(block, block, s_e, r_e.at[group], other)

    def gather(u):
        filtered_bytes(1, s_g, r_g.at[u]).wait_recv()
        a, b = split(f_all[u].T)
        for part in range(2):
            rows = slice(part * qw, (part + 1) * qw)
            ft[u, part, 0:qw, :] = a[rows]
            ft[u, part, qw:hw, :] = b[rows]

    def back_range(u, start, stop):
        @pl.loop(start, stop)
        def _(k):
            j = plane - k
            back(u, j)
            e_copy(u, j).start()

    def take_vals(h):
        all_vals(h).wait_recv()

        @pl.loop(1, plane)
        def _(j):
            q = peer(j)
            place_v(h, q, vals_all[h, q])

    def own_message():
        first = place * cells
        total_cells = cells * devices
        own_cols = columns(pos[...])
        same = lax.broadcasted_iota(jnp.int32, (slots, slots), 0) == lax.broadcasted_iota(
            jnp.int32, (slots, slots), 1
        )
        row_cell = lax.broadcasted_iota(jnp.int32, (slots, slots), 0) // cell
        col_cell = lax.broadcasted_iota(jnp.int32, (slots, slots), 1) // cell

        def listed(c, target):
            found = jnp.float32(0.0)
            for b in range(neigh.shape[1]):
                hit = (neigh[c, b] == target) & (b < ncount[c])
                found = found + jnp.where(hit, 1.0, 0.0)
            return found

        gathered = jnp.zeros((slots, width), F32)
        for shift in (-1, 0, 1):
            if shift:
                near_copy(0 if shift < 0 else 1).wait_recv()
            block = fm if shift == 0 else near.at[0 if shift < 0 else 1]
            where = block[slots:, 0:slots]
            atoms = block[0:slots, :]
            dist = jnp.zeros((slots, slots), F32)
            for axis in range(3):
                diff = own_cols[:, axis : axis + 1] - where[axis : axis + 1]
                dist = dist + diff * diff
            live = jnp.zeros((slots, slots), F32)
            for c in range(cells):
                for t in range(cells):
                    target = (first + shift * cells + t + total_cells) % total_cells
                    live = jnp.where((row_cell == c) & (col_cell == t), listed(c, target), live)
            weight = jnp.exp(-0.125 * dist) * live
            if shift == 0:
                weight = jnp.where(same, 0.0, weight)
            gathered = gathered + dot3(split(weight), split(atoms))
        msg[...] = feats[...] + 0.125 * dot3(split(gathered), split(w_late[0]))

    with scope("D_takeA"):
        take_vals(0)
    def at_inner(steps):
        @pl.when(inner)
        def _():
            for step, u, j in steps:
                step(u, j, True) if step is not finish_sum else step(u, j)

    def at_outer(steps):
        if nz > 2:

            @pl.when(outer)
            def _():
                for step, u, j in steps:
                    step(u, j, False)

    def sums(h, then=()):
        for j in range(nz):
            partial_sums(h, j)
            x_copy(h, j).start()
            if j > 1:
                at_outer([(send_sum, 2 * h, j - 2)])
            if j == nz // 2 - 1:
                at_inner(then)
        at_outer([(send_sum, 2 * h, j) for j in range(max(nz - 2, 0), nz)])
        at_outer([(send_sum, 2 * h + 1, j) for j in range(nz)])

    S, F, T = send_sum, finish_sum, take_filtered
    rest = list(range(1, side_z))

    def early(step, u):
        return [(step, u, 0 if step is not finish_sum else side_z)]

    def late(step, u):
        return [(step, u, j if step is not finish_sum else side_z + j) for j in rest]

    def own(u):
        return [(T, u, side_z)]

    def own_late(u):
        return [(T, u, side_z + j) for j in rest]

    cut = 1 + (plane - 1) // 3, 1 + 2 * (plane - 1) // 3

    with scope("D_psumA"):
        sums(0)
    with scope("D_send0"):
        at_inner(early(S, 0))
    start_near()
    start_on()
    with scope("E_takeB"):
        take_vals(1)
    with scope("E_psumB"):
        sums(1, late(S, 0))
    with scope("F_mid"):
        if nz > 2:

            @pl.when(inner)
            def _():
                filt_copy().wait_recv()

        at_inner(
            early(F, 0) + early(S, 1) + late(F, 0) + late(S, 1) + early(T, 0) + early(F, 1) + late(T, 0)
            + early(S, 2) + late(F, 1) + late(S, 2)
        )
        at_outer(own(0) + own_late(0) + early(T, 0) + own(1) + late(T, 0))
    pltpu.make_async_copy(w_late, w_late, s_late).wait()
    if nz > 2:
        with scope("F_msg"):

            @pl.when(outer)
            def _():
                own_message()

    with scope("G_gather0"):
        gather(0)
    with scope("G_back0"):
        back_range(0, 1, cut[1])
    with scope("G_a"):
        at_inner(early(T, 1) + early(F, 2) + late(T, 1) + early(S, 3) + late(F, 2) + late(S, 3))
        at_outer(own_late(1))
    with scope("G_back0"):
        back_range(0, cut[1], plane)
    with scope("G_b"):
        at_outer(early(T, 1) + own(2) + late(T, 1))
    with scope("G_gather1"):
        gather(1)
    with scope("G_back1"):
        back_range(1, 1, cut[0])
    with scope("G_c"):
        at_inner(early(T, 2) + early(F, 3) + late(T, 2) + late(F, 3))
        at_outer(own_late(2))
    with scope("G_back1"):
        back_range(1, cut[0], plane)
    with scope("G_d"):
        at_outer(early(T, 2) + own(3) + late(T, 2))
    with scope("G_gather2"):
        gather(2)
    with scope("G_back2"):
        back_range(2, 1, cut[0])
    with scope("G_e"):
        at_inner(early(T, 3))
    with scope("G_back2"):
        back_range(2, cut[0], cut[1])
    with scope("G_f"):
        at_inner(late(T, 3))
    with scope("G_back2"):
        back_range(2, cut[1], plane)
    with scope("K_take"):
        at_outer(own_late(3) + early(T, 3) + late(T, 3))
    with scope("K_msg"):

        @pl.when(inner)
        def _():
            own_message()

    with scope("K_gather3"):
        gather(3)
    with scope("K_back3"):
        back_range(3, 1, plane)
    with scope("K_own"):
        for u in range(pieces):
            back(u, 0)

    with scope("M_ewait"):
        for start, stop, group in ((0, pieces - 1, 0), (pieces - 1, pieces, 1)):
            all_e(start, stop, group).wait_recv()
            for u in range(start, stop):

                @pl.loop(1, plane)
                def _(j):
                    es[u, 0] = es[u, 0] + er[u, j]

    with scope("N_mlp"):
        summed = msg[...] + jnp.concatenate([es[u, 0] for u in range(pieces)], axis=0).T
        normed = summed / jnp.sqrt(jnp.mean(summed * summed, axis=1, keepdims=True) + 1e-06)
        v = dot3(split(normed), split(w_late[1]))
        hidden = v / (1.0 + jnp.exp(-v))
        result = summed + dot3(split(hidden), split(w_late[2]))
        for c in range(cells):
            part = slice(c * cell, (c + 1) * cell)
            out[part, :] = jnp.where(slot_ids < counts[c], result[part], 0.0)

    _sc = scope("O_waits")
    _sc.__enter__()
    block = kv_all.at[pl.ds(0, nz - 1)]
    rcopy(block, block, s_kv, r_kv.at[0], other).wait_send()
    all_pos().wait_send()
    all_vals(1).wait_send()
    rcopy(s_acc.at[:, :, 0], xbuf, s_x, r_x.at[0, 0], other).wait_send()
    filtered_bytes(pieces, s_g, r_g.at[0]).wait_send()
    all_e(0, pieces, 0).wait_send()

    @pl.when(inner)
    def _():
        block = zs.at[:, pl.ds(0, side_z)]
        rcopy(block, block, s_z, r_z.at[0, 0], other).wait_send()
        filtered_bytes(pieces * side_z // nz, s_f.at[0], r_f.at[0, 0]).wait_send()
        if nz > 2:
            filtered_bytes(pieces, s_f.at[1], r_f.at[0, 0]).wait_send()

    if nz > 2:

        @pl.when(outer)
        def _():
            rcopy(zs, zs, s_z, r_z.at[0, 0], other).wait_send()
            filt_copy().wait_send()

    for side, there in ((0, jnp.logical_not(at_high)), (1, jnp.logical_not(at_low))):

        @pl.when(there)
        def _():
            near_copy(side).wait_send()

    @pl.when(at_edge)
    def _():
        via_copy().wait_send()
        on_copy().wait_send()

    _sc.__exit__(None, None, None)


def shards(
    nz, feats, positions, cell_counts, neighbours, nbr_count, kvec, filters, w_msg, w_val, w_one, w_two
):
    slots, width = feats.shape
    kb = kvec.shape[1]
    waves = lax.axis_size("waves")
    plane = waves // nz
    devices = lax.axis_size("rows") * waves
    kpad = -(-nz * kb // 128) * 128
    kbpad = -(-kb // 128) * 128
    half = kb // 2
    hw = width // 2
    scale = 1.0 / math.sqrt(float(slots * devices) * float(kb * waves))
    natoms = plane * slots
    vm = pltpu.VMEM
    dma = pltpu.SemaphoreType.DMA
    any_spec = pl.BlockSpec(memory_space=pl.ANY)
    vmem_spec = pl.BlockSpec(memory_space=pltpu.VMEM)
    return pl.pallas_call(
        functools.partial(body, nz, plane, scale),
        out_shape=pltpu.VMEM((slots, width), F32),
        in_specs=[any_spec] * 11,
        out_specs=vmem_spec,
        scratch_shapes=[
            pltpu.SMEM(cell_counts.shape, jnp.int32),
            pltpu.SMEM(neighbours.shape, jnp.int32),
            pltpu.SMEM(nbr_count.shape, jnp.int32),
            vm((slots, width), F32),
            vm((3, slots), F32),
            vm((3, kb), F32),
            vm((kb, width), F32),
            vm((width, width), F32),
            vm((3, width, width), F32),
            vm((slots + 8, width), F32),
            vm((8, slots), F32),
            vm((8, kbpad), F32),
            vm((2, slots, hw), F32),
            vm((2, plane, slots, hw), F32),
            vm((plane, 8, slots), F32),
            vm((nz, 8, kbpad), F32),
            vm((2, slots + 8, width), F32),
            vm((slots + 8, width), F32),
            vm((kpad, 128), BF16),
            vm((kpad, natoms), BF16),
            vm((kpad, natoms), BF16),
            vm((kpad, natoms), BF16),
            vm((kpad, natoms), BF16),
            vm((2, natoms, width), BF16),
            vm((2, nz, 2, 2, half, hw), F32),
            vm((2, nz, 2, half, hw), F32),
            vm((4, nz, half, hw), F32),
            vm((2, 4, nz, half, hw), F32),
            vm((4, kpad, hw), F32),
            vm((4, 2, hw, kpad), BF16),
            vm((4, plane, hw // 2, slots), F32),
            vm((4, plane, hw // 2, slots), F32),
            vm((slots, width), F32),
            vm((half, width), F32),
            dma((8,)),
            dma(()),
            dma(()),
            dma(()),
            dma((2,)),
            dma((2,)),
            dma((2,)),
            dma((2,)),
            dma(()),
            dma(()),
            dma(()),
            dma(()),
            dma((nz,)),
            dma(()),
            dma((2, nz)),
            dma(()),
            dma((5, nz)),
            dma((2,)),
            dma((5, nz)),
            dma(()),
            dma((4,)),
            dma(()),
            dma((2,)),
            dma((1,)),
            dma((1,)),
        ],
        compiler_params=pltpu.CompilerParams(collective_id=0, has_side_effects=True),
        name="ewald_layer",
    )(cell_counts, neighbours, nbr_count, feats, positions, kvec, filters, w_msg, w_val, w_one, w_two)


def solution(mesh):
    nz = 4 if mesh.shape["waves"] % 4 == 0 else 2
    placed = (
        P(("rows", "waves"), None),
        P(None, ("rows", "waves")),
        P(("rows", "waves")),
        P(("rows", "waves"), None),
        P(("rows", "waves")),
        P(None, "waves"),
        P("waves", None),
        P(),
        P(),
        P(),
        P(),
    )
    return jax.shard_map(
        functools.partial(shards, nz),
        mesh=mesh,
        in_specs=placed,
        out_specs=P(("rows", "waves"), None),
        check_vma=False,
    )
```

```python
import functools
import math

import jax
import jax.numpy as jnp
from jax import lax
from jax.experimental import pallas as pl
from jax.experimental.pallas import tpu as pltpu
from jax.sharding import PartitionSpec as P

MESH = pl.DeviceIdType.MESH
F32 = jnp.float32
BF16 = jnp.bfloat16

SIN = (4.44286798, -7.30744541, 3.5948021, -0.78440363)
COS = (1.4142135, -6.97885099, 5.73946117, -1.88356299, 0.31069819)


def split(x):
    high = x.astype(BF16)
    return high, (x - high.astype(F32)).astype(BF16)


def split3(x):
    a = x.astype(BF16).astype(F32)
    rest = x - a
    b = rest.astype(BF16).astype(F32)
    return a, b, rest - b


def mm(a, b):
    return jnp.dot(a, b, preferred_element_type=F32)


def dot3(a, b):
    return mm(a[0], b[0]) + mm(a[0], b[1]) + mm(a[1], b[0])


def horner(y, coefficients):
    total = y * coefficients[-1] + coefficients[-2]
    for coefficient in coefficients[-3::-1]:
        total = total * y + coefficient
    return total


def sincos(turns):
    x = turns - jnp.round(turns)
    y = x * x
    s = x * horner(y, SIN)
    c = horner(y, COS)
    return s * c, 1.0 - s * s


def columns(rows):
    height, width = rows.shape
    return jnp.concatenate([rows, jnp.zeros((128 - height, width), F32)], axis=0).T


def body(
    nz, plane, scale,
    counts_in, neigh_in, ncount_in, feats_in, pos_in, kv_in, filt_in, w_msg_in, w_val_in, w_one_in, w_two_in,
    out,
    counts, neigh, ncount, feats, pos3, kv3, filt, w_val, w_late,
    fm, pos, kv, vals, vals_all, pos_all, kv_all, near, via, km, ch, cl, sh, sl, fcat,
    s_acc, xbuf, zs, zr, f_all, ft, es, er, msg, filt_far, w_split,
    s_in, s_late, s_pos, r_pos, s_val, r_val, s_near, r_near, s_via, r_via, s_on, s_kv, r_kv, s_x, r_x, s_z, r_z, s_f, r_f, s_g, r_g, s_e, r_e, s_filt, r_filt,
):
    slots, width = feats.shape
    kb = filt.shape[0]
    half = kb // 2
    hw = width // 2
    qw = hw // 2
    pieces = 4
    kall = nz * kb
    kpad = km.shape[0]
    cells = counts.shape[0]
    cell = slots // cells
    waves = nz * plane
    r = lax.axis_index("rows")
    w = lax.axis_index("waves")
    z = w // plane
    p = w % plane
    other = (1 - r, w)
    place = r * waves + w
    devices = 2 * waves
    scope = jax.named_scope
    at_low = p == 0
    at_high = p == plane - 1
    at_edge = at_low | at_high
    facing = z * plane + plane - 1 - p
    met = at_edge & ((z == 0) | (z == nz - 1))

    def plane_dev(j):
        return (r, z * plane + (p + j) % plane)

    bits = (plane - 1).bit_length()

    def peer(j):
        q = p
        for b in range(bits):
            q = q + ((j // (1 << b)) % 2) * (1 << b) * (1 - 2 * ((p // (1 << b)) % 2))
        return q

    def peer_dev(j):
        return (r, z * plane + peer(j))

    def z_dev(j):
        return (r, ((z + j) % nz) * plane + p)

    def rcopy(src, dst, ssem, rsem, dev):
        return pltpu.make_async_remote_copy(
            src_ref=src, dst_ref=dst, send_sem=ssem, recv_sem=rsem, device_id=dev, device_id_type=MESH
        )

    def rows_of(block):
        return pl.ds(pl.multiple_of(block * slots, slots), slots)

    loads = [
        pltpu.make_async_copy(src, dst, s_in.at[i])
        for i, (src, dst) in enumerate(
            (
                (pos_in, pos3),
                (kv_in, kv3),
                (feats_in, feats),
                (w_val_in, w_val),
                (filt_in, filt),
                (counts_in, counts),
                (neigh_in, neigh),
                (ncount_in, ncount),
            )
        )
    ]
    late_loads = [
        pltpu.make_async_copy(src, w_late.at[i], s_late) for i, src in enumerate((w_msg_in, w_one_in, w_two_in))
    ]
    for load in loads + late_loads:
        load.start()

    natoms = plane * slots
    lower = z < nz // 2
    rank = jnp.where(lower, z, nz - 1 - z)
    side_z = nz // 2
    inner = rank == side_z - 1
    outer = jnp.logical_not(inner)
    sign = jnp.where(lower, 1, -1)
    toward = (r, (z + sign) * plane + p)
    away = (r, (z - sign) * plane + p)

    def block_at(j):
        block = nz - 1 - j if j < side_z else j - side_z
        return jnp.where(lower, block, nz - 1 - block)

    mine = pl.multiple_of(r * half, 8)

    barrier = pltpu.get_barrier_semaphore()
    pl.semaphore_signal(barrier, inc=1, device_id=other, device_id_type=MESH)

    @pl.when(met)
    def _():
        pl.semaphore_signal(barrier, inc=1, device_id=(1 - r, facing), device_id_type=MESH)

    for j in range(1, nz):
        pl.semaphore_signal(barrier, inc=1, device_id=z_dev(j), device_id_type=MESH)

    @pl.loop(1, plane)
    def _(j):
        pl.semaphore_signal(barrier, inc=1, device_id=plane_dev(j), device_id_type=MESH)

    with scope("A_load"):
        loads[0].wait()
        loads[1].wait()
        pos[...] = jnp.zeros_like(pos)
        pos[0:3, :] = pos3[...]
        kv[...] = jnp.zeros_like(kv)
        kv[0:3, 0:kb] = kv3[...] * (0.5 / math.pi)
    with scope("A_barrier"):
        pl.semaphore_wait(barrier, nz + plane - 1 + jnp.where(met, 1, 0))

    def kv_copy(j):
        return rcopy(kv, kv_all.at[z], s_kv, r_kv.at[z], z_dev(j))

    def kv_arrival(j):
        q = (z + j) % nz
        return rcopy(kv, kv_all.at[q], s_kv, r_kv.at[q], z_dev(j))

    def pos_copy(j):
        return rcopy(pos, pos_all.at[p], s_pos, r_pos, peer_dev(j))

    def val_copy(h, j):
        return rcopy(vals.at[h], vals_all.at[h, p], s_val.at[h], r_val.at[h], peer_dev(j))

    def all_pos():
        block = pos_all.at[pl.ds(0, plane - 1)]
        return rcopy(block, block, s_pos, r_pos, other)

    def all_vals(h):
        block = vals_all.at[h, pl.ds(0, plane - 1)]
        return rcopy(block, block, s_val.at[h], r_val.at[h], other)

    def near_copy(side):
        dev = plane_dev(1 if side == 0 else plane - 1)
        return rcopy(fm, near.at[side], s_near.at[side], r_near.at[side], dev)

    def via_copy():
        dev = (r, ((z + jnp.where(at_high, 1, nz - 1)) % nz) * plane + p)
        return rcopy(fm, via, s_via, r_via, dev)

    def on_copy():
        side = jnp.where(at_high, 0, 1)
        flip = (at_high & (z == 0)) | (at_low & (z == nz - 1))
        dev = (jnp.where(flip, 1 - r, r), facing)
        return rcopy(via, near.at[side], s_on, r_near.at[side], dev)

    def start_near():
        for side, there in ((0, jnp.logical_not(at_high)), (1, jnp.logical_not(at_low))):

            @pl.when(there)
            def _():
                near_copy(side).start()

    def start_on():
        @pl.when(at_edge)
        def _():
            via_copy().wait_recv()
            on_copy().start()

    def filt_copy():
        return rcopy(filt.at[pl.ds(mine, half), :], filt_far, s_filt.at[0], r_filt.at[0], toward)

    for j in range(1, nz):
        kv_copy(j).start()

    @pl.loop(1, plane)
    def _(j):
        pos_copy(j).start()

    slot_ids = lax.broadcasted_iota(jnp.int32, (cell, width), 0)
    with scope("B_project"):
        loads[2].wait()
        for load in loads[5:]:
            load.wait()
        for c in range(cells):
            part = slice(c * cell, (c + 1) * cell)
            fm[part, :] = jnp.where(slot_ids < counts[c], feats[part, :], 0.0)
        fm[slots:, 0:slots] = pos[...]
        loads[3].wait()
        projected = dot3(split(fm[0:slots, :]), split(w_val[...]))
        for h in range(2):
            vals[h] = projected[:, h * hw : (h + 1) * hw]

    @pl.loop(1, plane)
    def _(j):
        val_copy(0, plane - j).start()

    loads[4].wait()
    if nz > 2:

        @pl.when(outer)
        def _():
            filt_copy().start()

    def place_k(block, rows):
        a, b, c = split3(rows)
        stack = [a, a, a, b, b, b, c, c, c]
        stack.append(jnp.zeros((128 - 8 * len(stack), rows.shape[1]), F32))
        km[pl.ds(pl.multiple_of(block * kb, 16), kb), :] = jnp.concatenate(stack, axis=0).T[:kb].astype(BF16)

    def place_v(h, q, block):
        a, b = split(block)
        fcat[h, rows_of(q), 0:hw] = a
        fcat[h, rows_of(q), hw:width] = b

    if kpad > kall:
        f_all[:, kall:, :] = jnp.zeros((pieces, kpad - kall, hw), F32)
    for h in range(2):
        place_v(h, p, vals[h])
    with scope("B_kv"):
        place_k(z, kv[...])
        if kpad > kall:
            km[kall:, :] = jnp.zeros((kpad - kall, 128), BF16)
        for j in [1, nz - 1] + list(range(2, nz - 1)) if nz > 2 else [1]:
            kv_arrival(j).wait_recv()
            if j == nz - 1:

                @pl.when(at_edge)
                def _():
                    via_copy().start()

            q = (z + j) % nz
            place_k(q, kv_all[q])

    def phases(q, rows3):
        stack = list(split3(rows3)) * 3
        stack.append(jnp.zeros((128 - 8 * len(stack), slots), F32))
        s, c = sincos(mm(km[...], jnp.concatenate(stack, axis=0).astype(BF16)))
        lanes = rows_of(q)
        a, b = split(c)
        ch[:, lanes] = a
        cl[:, lanes] = b
        a, b = split(s)
        sh[:, lanes] = a
        sl[:, lanes] = b

    pos_all[p] = pos[...]

    with scope("C_phases"):

        @pl.loop(0, plane)
        def _(j):
            q = peer(j)

            @pl.when(j == 1)
            def _():
                with scope("c_poswait"):
                    all_pos().wait_recv()

            with scope("c_phase"):
                phases(q, pos_all[q])

            @pl.when(j == plane // 2)
            def _():
                all_vals(0).wait_send()

                @pl.loop(1, plane)
                def _(k):
                    val_copy(1, plane - k).start()


    def partial_sums(h, j):
        zb = block_at(j)
        ks = pl.ds(pl.multiple_of(zb * kb, 16), kb)
        totals = []
        for hi, lo in ((ch, cl), (sh, sl)):
            wide = mm(hi[ks, :], fcat[h])
            totals.append(wide[:, :hw] + wide[:, hw:] + mm(lo[ks, :], fcat[h, :, 0:hw]))
        for i in range(2):
            piece = jnp.concatenate([total[:, i * qw : (i + 1) * qw] for total in totals], axis=1)
            for c in range(2):
                s_acc[h, zb, c, i] = piece[c * half : (c + 1) * half]

    def x_copy(h, j):
        zb = block_at(j)
        return rcopy(s_acc.at[h, zb, 1 - r], xbuf.at[h, zb], s_x, r_x.at[h, zb], other)

    def units(u):
        if u < pieces - 1 or half % 16:
            return [(u, slice(0, half))]
        return [(u, slice(0, half // 2)), (u + 1, slice(half // 2, half))]

    def s_hop(u, j, source, unit):
        zb = block_at(j)
        index, rows = unit
        return rcopy(zs.at[u, zb, rows], zr.at[source, u, zb, rows], s_z, r_f.at[index, zb] if source else r_z.at[index, zb], toward)

    def gathered_sum(u, j, sources, unit):
        zb = block_at(j)
        rows = unit[1]
        total = s_acc[u // 2, zb, r, u % 2, rows, :] + xbuf[u // 2, zb, u % 2, rows, :]
        for source in sources:
            s_hop(u, j, source, unit).wait_recv()
            total = total + zr[source, u, zb, rows, :]
        return total

    def send_sum(u, j, is_inner):
        if u % 2 == 0:
            x_copy(u // 2, j).wait_recv()
        for unit in units(u):
            zs[u, block_at(j), unit[1], :] = gathered_sum(u, j, (0,) if is_inner and nz > 2 else (), unit)
            s_hop(u, j, 1 if is_inner else 0, unit).start()

    def share(u, zb, rows):
        start = pl.multiple_of((zb * 2 + r) * half + rows.start, 8)
        return f_all.at[u, pl.ds(start, rows.stop - rows.start), :]

    def f_hop(u, zb, way, dev, unit):
        here = share(u, zb, unit[1])
        return rcopy(here, here, s_f.at[way], r_f.at[unit[0], zb], dev)

    def f_relay(u, zb, unit):
        here = share(u, zb, unit[1])
        return rcopy(here, here, s_g, r_g.at[u], other)

    def filtered_bytes(pieces_sent, ssem, rsem):
        block = f_all.at[pl.ds(0, pieces_sent), pl.ds(0, nz * half)]
        return rcopy(block, block, ssem, rsem, other)

    def finish_sum(u, j):
        zb = block_at(j)
        lanes = slice(u * qw, (u + 1) * qw)
        kept = filt[pl.ds(mine, half), lanes] if j == nz - 1 else filt_far[:, lanes]
        kept = jnp.concatenate([kept, kept], axis=1) * scale
        if u % 2 == 0:
            x_copy(u // 2, j).wait_recv()
        for unit in units(u):
            rows = unit[1]
            total = gathered_sum(u, j, (0, 1) if nz > 2 else (1,), unit)
            start = pl.multiple_of((zb * 2 + r) * half + rows.start, 8)
            f_all[u, pl.ds(start, rows.stop - rows.start), :] = kept[rows] * total
            f_hop(u, zb, 0, toward, unit).start()
            if nz > 2:
                f_hop(u, zb, 1, away, unit).start()
            f_relay(u, zb, unit).start()

    def take_filtered(u, j, is_inner):
        zb = block_at(j)
        for unit in units(u):
            f_hop(u, zb, 0, other, unit).wait_recv()
            if is_inner and nz > 2:
                f_hop(u, zb, 1, away, unit).start()
            f_relay(u, zb, unit).start()

    def back(u, j):
        lanes = rows_of(peer(j))
        total = jnp.zeros((qw, slots), F32)
        for part, (hi, lo) in enumerate(((ch, cl), (sh, sl))):
            both = mm(ft[u, part], hi[:, lanes])
            total = total + both[:qw] + both[qw:] + mm(ft[u, part, 0:qw, :], lo[:, lanes])
        es[u, j] = total

    def e_copy(u, j):
        return rcopy(es.at[u, j], er.at[u, j], s_e, r_e.at[u // (pieces - 1)], peer_dev(j))

    def all_e(start, stop, group):
        block = er.at[pl.ds(start, stop - start), pl.ds(1, plane - 1)]
        return rcopy(block, block, s_e, r_e.at[group], other)

    def gather(u):
        filtered_bytes(1, s_g, r_g.at[u]).wait_recv()
        a, b = split(f_all[u].T)
        for part in range(2):
            rows = slice(part * qw, (part + 1) * qw)
            ft[u, part, 0:qw, :] = a[rows]
            ft[u, part, qw:hw, :] = b[rows]

    def back_range(u, start, stop):
        @pl.loop(start, stop)
        def _(k):
            j = plane - k
            back(u, j)
            e_copy(u, j).start()

    def take_vals(h):
        all_vals(h).wait_recv()

        @pl.loop(1, plane)
        def _(j):
            q = peer(j)
            place_v(h, q, vals_all[h, q])

    def own_message():
        first = place * cells
        total_cells = cells * devices
        own_cols = columns(pos[...])
        same = lax.broadcasted_iota(jnp.int32, (slots, slots), 0) == lax.broadcasted_iota(
            jnp.int32, (slots, slots), 1
        )
        row_cell = lax.broadcasted_iota(jnp.int32, (slots, slots), 0) // cell
        col_cell = lax.broadcasted_iota(jnp.int32, (slots, slots), 1) // cell

        def listed(c, target):
            found = jnp.float32(0.0)
            for b in range(neigh.shape[1]):
                hit = (neigh[c, b] == target) & (b < ncount[c])
                found = found + jnp.where(hit, 1.0, 0.0)
            return found

        gathered = jnp.zeros((slots, width), F32)
        for shift in (-1, 0, 1):
            if shift:
                near_copy(0 if shift < 0 else 1).wait_recv()
            block = fm if shift == 0 else near.at[0 if shift < 0 else 1]
            where = block[slots:, 0:slots]
            atoms = block[0:slots, :]
            dist = jnp.zeros((slots, slots), F32)
            for axis in range(3):
                diff = own_cols[:, axis : axis + 1] - where[axis : axis + 1]
                dist = dist + diff * diff
            live = jnp.zeros((slots, slots), F32)
            for c in range(cells):
                for t in range(cells):
                    target = (first + shift * cells + t + total_cells) % total_cells
                    live = jnp.where((row_cell == c) & (col_cell == t), listed(c, target), live)
            weight = jnp.exp(-0.125 * dist) * live
            if shift == 0:
                weight = jnp.where(same, 0.0, weight)
            gathered = gathered + dot3(split(weight), split(atoms))
        msg[...] = feats[...] + 0.125 * dot3(split(gathered), split(w_late[0]))

    with scope("D_takeA"):
        take_vals(0)
    def at_inner(steps):
        @pl.when(inner)
        def _():
            for step, u, j in steps:
                step(u, j, True) if step is not finish_sum else step(u, j)

    def at_outer(steps):
        if nz > 2:

            @pl.when(outer)
            def _():
                for step, u, j in steps:
                    step(u, j, False)

    def sums(h, then=()):
        for j in range(nz):
            partial_sums(h, j)
            x_copy(h, j).start()
            if j > 1:
                at_outer([(send_sum, 2 * h, j - 2)])
            if j == nz // 2 - 1:
                at_inner(then)
        at_outer([(send_sum, 2 * h, j) for j in range(max(nz - 2, 0), nz)])
        at_outer([(send_sum, 2 * h + 1, j) for j in range(nz)])

    S, F, T = send_sum, finish_sum, take_filtered
    rest = list(range(1, side_z))

    def early(step, u):
        return [(step, u, 0 if step is not finish_sum else side_z)]

    def late(step, u):
        return [(step, u, j if step is not finish_sum else side_z + j) for j in rest]

    def own(u):
        return [(T, u, side_z)]

    def own_late(u):
        return [(T, u, side_z + j) for j in rest]

    cut = 1 + (plane - 1) // 3, 1 + 2 * (plane - 1) // 3

    with scope("D_psumA"):
        sums(0)
    with scope("D_send0"):
        at_inner(early(S, 0))
    start_near()
    start_on()
    with scope("E_takeB"):
        take_vals(1)
    with scope("E_psumB"):
        sums(1, late(S, 0))
    with scope("F_mid"):
        if nz > 2:

            @pl.when(inner)
            def _():
                filt_copy().wait_recv()

        at_inner(
            early(F, 0) + early(S, 1) + late(F, 0) + late(S, 1) + early(T, 0) + early(F, 1) + early(S, 2) + late(T, 0) + late(F, 1) + late(S, 2)
        )
        at_outer(own(0) + own_late(0) + early(T, 0) + own(1) + late(T, 0))
    pltpu.make_async_copy(w_late, w_late, s_late).wait()
    if nz > 2:
        with scope("F_msg"):

            @pl.when(outer)
            def _():
                own_message()

    with scope("G_gather0"):
        gather(0)
    with scope("G_back0"):
        back_range(0, 1, cut[1])
    with scope("G_a"):
        at_inner(early(T, 1) + early(F, 2) + early(S, 3) + late(T, 1) + late(F, 2) + late(S, 3))
        at_outer(own_late(1))
    with scope("G_back0"):
        back_range(0, cut[1], plane)
    with scope("G_b"):
        at_outer(early(T, 1) + own(2) + late(T, 1))
    with scope("G_gather1"):
        gather(1)
    with scope("G_back1"):
        back_range(1, 1, cut[0])
    with scope("G_c"):
        at_inner(early(T, 2) + early(F, 3) + late(T, 2) + late(F, 3))
        at_outer(own_late(2))
    with scope("G_back1"):
        back_range(1, cut[0], plane)
    with scope("G_d"):
        at_outer(early(T, 2) + own(3) + late(T, 2))
    with scope("G_gather2"):
        gather(2)
    with scope("G_back2"):
        back_range(2, 1, cut[0])
    with scope("G_e"):
        at_inner(early(T, 3))
    with scope("G_back2"):
        back_range(2, cut[0], cut[1])
    with scope("G_f"):
        at_inner(late(T, 3))
    with scope("G_back2"):
        back_range(2, cut[1], plane)
    with scope("K_take"):
        at_outer(own_late(3) + early(T, 3) + late(T, 3))
    with scope("K_msg"):

        @pl.when(inner)
        def _():
            own_message()

    with scope("K_gather3"):
        gather(3)
    with scope("K_back3"):
        back_range(3, 1, plane)
    final = pieces - 1
    with scope("K_own"):
        for u in range(pieces):
            back(u, 0)
        for i in range(2):
            for k, piece in enumerate(split(w_late[i + 1])):
                w_split[i, k] = piece

    def add_arrivals(u):
        @pl.loop(1, plane)
        def _(j):
            es[u, 0] = es[u, 0] + er[u, j]

    with scope("M_pre"):
        all_e(0, final, 0).wait_recv()
        for u in range(final):
            add_arrivals(u)
        msg[:, 0:hw] = msg[:, 0:hw] + jnp.concatenate([es[0, 0], es[1, 0]], axis=0).T
    with scope("M_ewait"):
        all_e(final, pieces, 1).wait_recv()
        add_arrivals(final)

    with scope("N_mlp"):
        right = msg[:, hw:width] + jnp.concatenate([es[2, 0], es[3, 0]], axis=0).T
        summed = jnp.concatenate([msg[:, 0:hw], right], axis=1)
        normed = summed / jnp.sqrt(jnp.mean(summed * summed, axis=1, keepdims=True) + 1e-06)
        v = dot3(split(normed), (w_split[0, 0], w_split[0, 1]))
        hidden = v / (1.0 + jnp.exp(-v))
        result = summed + dot3(split(hidden), (w_split[1, 0], w_split[1, 1]))
        for c in range(cells):
            part = slice(c * cell, (c + 1) * cell)
            out[part, :] = jnp.where(slot_ids < counts[c], result[part], 0.0)

    _sc = scope("O_waits")
    _sc.__enter__()
    block = kv_all.at[pl.ds(0, nz - 1)]
    rcopy(block, block, s_kv, r_kv.at[0], other).wait_send()
    all_pos().wait_send()
    all_vals(1).wait_send()
    rcopy(s_acc.at[:, :, 0], xbuf, s_x, r_x.at[0, 0], other).wait_send()
    filtered_bytes(pieces, s_g, r_g.at[0]).wait_send()
    all_e(0, pieces, 0).wait_send()

    @pl.when(inner)
    def _():
        block = zs.at[:, pl.ds(0, side_z)]
        rcopy(block, block, s_z, r_z.at[0, 0], other).wait_send()
        filtered_bytes(pieces * side_z // nz, s_f.at[0], r_f.at[0, 0]).wait_send()
        if nz > 2:
            filtered_bytes(pieces, s_f.at[1], r_f.at[0, 0]).wait_send()

    if nz > 2:

        @pl.when(outer)
        def _():
            rcopy(zs, zs, s_z, r_z.at[0, 0], other).wait_send()
            filt_copy().wait_send()

    for side, there in ((0, jnp.logical_not(at_high)), (1, jnp.logical_not(at_low))):

        @pl.when(there)
        def _():
            near_copy(side).wait_send()

    @pl.when(at_edge)
    def _():
        via_copy().wait_send()
        on_copy().wait_send()

    _sc.__exit__(None, None, None)


def shards(
    nz, feats, positions, cell_counts, neighbours, nbr_count, kvec, filters, w_msg, w_val, w_one, w_two
):
    slots, width = feats.shape
    kb = kvec.shape[1]
    waves = lax.axis_size("waves")
    plane = waves // nz
    devices = lax.axis_size("rows") * waves
    kpad = -(-nz * kb // 128) * 128
    kbpad = -(-kb // 128) * 128
    half = kb // 2
    hw = width // 2
    scale = 1.0 / math.sqrt(float(slots * devices) * float(kb * waves))
    natoms = plane * slots
    vm = pltpu.VMEM
    dma = pltpu.SemaphoreType.DMA
    any_spec = pl.BlockSpec(memory_space=pl.ANY)
    vmem_spec = pl.BlockSpec(memory_space=pltpu.VMEM)
    return pl.pallas_call(
        functools.partial(body, nz, plane, scale),
        out_shape=pltpu.VMEM((slots, width), F32),
        in_specs=[any_spec] * 11,
        out_specs=vmem_spec,
        scratch_shapes=[
            pltpu.SMEM(cell_counts.shape, jnp.int32),
            pltpu.SMEM(neighbours.shape, jnp.int32),
            pltpu.SMEM(nbr_count.shape, jnp.int32),
            vm((slots, width), F32),
            vm((3, slots), F32),
            vm((3, kb), F32),
            vm((kb, width), F32),
            vm((width, width), F32),
            vm((3, width, width), F32),
            vm((slots + 8, width), F32),
            vm((8, slots), F32),
            vm((8, kbpad), F32),
            vm((2, slots, hw), F32),
            vm((2, plane, slots, hw), F32),
            vm((plane, 8, slots), F32),
            vm((nz, 8, kbpad), F32),
            vm((2, slots + 8, width), F32),
            vm((slots + 8, width), F32),
            vm((kpad, 128), BF16),
            vm((kpad, natoms), BF16),
            vm((kpad, natoms), BF16),
            vm((kpad, natoms), BF16),
            vm((kpad, natoms), BF16),
            vm((2, natoms, width), BF16),
            vm((2, nz, 2, 2, half, hw), F32),
            vm((2, nz, 2, half, hw), F32),
            vm((4, nz, half, hw), F32),
            vm((2, 4, nz, half, hw), F32),
            vm((4, kpad, hw), F32),
            vm((4, 2, hw, kpad), BF16),
            vm((4, plane, hw // 2, slots), F32),
            vm((4, plane, hw // 2, slots), F32),
            vm((slots, width), F32),
            vm((half, width), F32),
            vm((2, 2, width, width), BF16),
            dma((8,)),
            dma(()),
            dma(()),
            dma(()),
            dma((2,)),
            dma((2,)),
            dma((2,)),
            dma((2,)),
            dma(()),
            dma(()),
            dma(()),
            dma(()),
            dma((nz,)),
            dma(()),
            dma((2, nz)),
            dma(()),
            dma((5, nz)),
            dma((2,)),
            dma((5, nz)),
            dma(()),
            dma((4,)),
            dma(()),
            dma((2,)),
            dma((1,)),
            dma((1,)),
        ],
        compiler_params=pltpu.CompilerParams(collective_id=0, has_side_effects=True),
        name="ewald_layer",
    )(cell_counts, neighbours, nbr_count, feats, positions, kvec, filters, w_msg, w_val, w_one, w_two)


def solution(mesh):
    nz = 4 if mesh.shape["waves"] % 4 == 0 else 2
    placed = (
        P(("rows", "waves"), None),
        P(None, ("rows", "waves")),
        P(("rows", "waves")),
        P(("rows", "waves"), None),
        P(("rows", "waves")),
        P(None, "waves"),
        P("waves", None),
        P(),
        P(),
        P(),
        P(),
    )
    return jax.shard_map(
        functools.partial(shards, nz),
        mesh=mesh,
        in_specs=placed,
        out_specs=P(("rows", "waves"), None),
        check_vma=False,
    )
```
